32 devices in a mesh: ctx: 8 (over y, x, core), fsdp: 4 (over z).
Axes of the slice: x: 2, y: 2, z: 4, core: 2. Of those that a mesh axis runs over, the one named last changes fastest.
Arguments:
- tokens: bfloat16 [4, 2048, 768], P(None, ('ctx', 'fsdp')), may hold values from -6 to 6
- cotangent: bfloat16 [4, 2048, 768], P(None, ('ctx', 'fsdp')), may hold values from -6 to 6
- time_index: int32 [4], replicated, may hold values from 0 to 255
- absorbed: int32 [4, 2048], P(None, ('ctx', 'fsdp')), may hold values 0 or 1
- time_table: bfloat16 [256, 128], P('fsdp'), may hold values from -6 to 6
- ada_weight: bfloat16 [128, 4608], P('fsdp'), may hold values from -0.5 to 0.5
- ada_bias: bfloat16 [4608], P('fsdp'), may hold values from -4 to 4
- attn_gain: bfloat16 [768], P('fsdp'), may hold values from 0.25 to 1.75
- qkv_weight: bfloat16 [768, 2304], P('fsdp'), may hold values from -0.21875 to 0.21875
- out_weight: bfloat16 [768, 768], P('fsdp'), may hold values from -6 to 6
- mlp_gain: bfloat16 [768], P('fsdp'), may hold values from 0.25 to 1.75
- up_weight: bfloat16 [768, 3072], P('fsdp'), may hold values from -0.21875 to 0.21875
- up_bias: bfloat16 [3072], P('fsdp'), may hold values from -4 to 4
- down_weight: bfloat16 [3072, 768], P('fsdp'), may hold values from -0.109375 to 0.109375
- down_bias: bfloat16 [768], P('fsdp'), may hold values from -6 to 6
- mask_vector: bfloat16 [768], P('fsdp'), may hold values from -6 to 6
Outputs:
- output: float32 [4, 2048, 768], P(None, ('ctx', 'fsdp'))
- grad_tokens: float32 [4, 2048, 768], P(None, ('ctx', 'fsdp'))
- grad_table: float32 [256, 128], P(('ctx', 'fsdp'))
- grad_ada_weight: float32 [128, 4608], P(('ctx', 'fsdp'))
- grad_ada_bias: float32 [4608], P(('ctx', 'fsdp'))
- grad_attn_gain: float32 [768], P(('ctx', 'fsdp'))
- grad_qkv_weight: float32 [768, 2304], P(('ctx', 'fsdp'))
- grad_out_weight: float32 [768, 768], P(('ctx', 'fsdp'))
- grad_mlp_gain: float32 [768], P(('ctx', 'fsdp'))
- grad_up_weight: float32 [768, 3072], P(('ctx', 'fsdp'))
- grad_up_bias: float32 [3072], P(('ctx', 'fsdp'))
- grad_down_weight: float32 [3072, 768], P(('ctx', 'fsdp'))
- grad_down_bias: float32 [768], P(('ctx', 'fsdp'))
- grad_mask_vector: float32 [768], P(('ctx', 'fsdp'))
The draws below stay inside these ranges and needn't reach their ends.
All inputs are finite; a program needn't handle non-finite values. No bound on the sum of `absorbed` on one device may be relied on, other than what follows from the above.
Results may differ from the reference program's by a relative error of at most 0.015.
Values may be sent and summed in bfloat16 or wider, within the bound.
No kernel may reach another device: no remote copies, remote signals or barrier semaphores. Data moves between devices by JAX's collectives and lax.ppermute only.
A program may use at most 320 MiB of HBM per device.

```python
import math
import jax
import jax.numpy as jnp
from jax import lax

D = 768
H = 12
HD = 64
FF = 3072
C = 128
STEPS = 256
B = 4
SEQ = 2048


def set_ends(values, rng, smallest, high):
    index_at = [jax.random.randint(jax.random.fold_in(rng, axis), (), 0, length) for axis, length in enumerate(values.shape)]
    main_axis = values.shape.index(max(values.shape))
    next_to = index_at[:main_axis] + [(index_at[main_axis] + 1) % values.shape[main_axis]] + index_at[main_axis + 1:]
    return values.at[tuple(index_at)].set(smallest).at[tuple(next_to)].set(high)


def steps_of(rng, dims, split, low, high):
    gain, own = 1.0, jax.random.fold_in(rng, 6)
    for position, blocks in split:
        steps = jnp.exp(jax.random.uniform(jax.random.fold_in(own, position), (blocks,), jnp.float32, low / len(split), high / len(split)))
        gain = gain * jnp.repeat(steps, dims[position] // blocks).reshape([-1 if axis == position else 1 for axis in range(len(dims))])
    return gain


def scatter_about(own_key, extent, scale, reach, split=(), kind=jnp.bfloat16):
    loudness = steps_of(own_key, extent, split, -0.22, 0.18) if split else 1.0
    result = jax.random.normal(own_key, extent, jnp.float32) * scale * loudness
    return jnp.minimum(jnp.maximum(result, -reach), reach).astype(kind)


def setup_inputs(seed: int = 0) -> dict:
    key_of = jax.random.split(jax.random.key(seed), 17)
    return {
        "tokens": scatter_about(key_of[0], (B, SEQ, D), 1.0, 6.0, ((1, 32),)),
        "cotangent": scatter_about(key_of[1], (B, SEQ, D), 1.0, 6.0, ((1, 32),)),
        "time_index": set_ends(jax.random.randint(key_of[2], (B,), 0, STEPS), jax.random.fold_in(key_of[2], 1), 0, STEPS - 1).astype(jnp.int32),
        "absorbed": set_ends((jax.random.randint(key_of[3], (B, SEQ), 0, 4) < 1).astype(jnp.int32), jax.random.fold_in(key_of[3], 1), 0, 1),
        "time_table": scatter_about(key_of[4], (STEPS, C), 1.0, 6.0, ((0, 4),)),
        "ada_weight": scatter_about(key_of[5], (C, 6 * D), C ** -0.5, 0.5, ((0, 4),)),
        "ada_bias": scatter_about(key_of[6], (6 * D,), 0.3, 4.0, ((0, 4),)),
        "attn_gain": jnp.clip(1.0 + 0.15 * jax.random.normal(key_of[7], (D,), jnp.float32), 0.25, 1.75).astype(jnp.bfloat16),
        "qkv_weight": scatter_about(key_of[8], (D, 3 * D), D ** -0.5, 0.21875, ((0, 4),)),
        "out_weight": scatter_about(key_of[9], (D, D), (max(1, 3 * D // SEQ)) ** -0.5, 6.0, ((0, 4),)),
        "mlp_gain": jnp.clip(1.0 + 0.15 * jax.random.normal(key_of[10], (D,), jnp.float32), 0.25, 1.75).astype(jnp.bfloat16),
        "up_weight": scatter_about(key_of[11], (D, FF), D ** -0.5, 0.21875, ((0, 4),)),
        "up_bias": scatter_about(key_of[12], (FF,), 0.3, 4.0, ((0, 4),)),
        "down_weight": scatter_about(key_of[13], (FF, D), FF ** -0.5, 0.109375, ((0, 4),)),
        "down_bias": scatter_about(key_of[14], (D,), 0.8, 6.0, ((0, 4),)),
        "mask_vector": scatter_about(key_of[15], (D,), 1.0, 6.0, ((0, 4),)),
    }


@jax.custom_vjp
def low(v):
    return lax.optimization_barrier(v.astype(jnp.bfloat16)).astype(jnp.float32)

@jax.custom_vjp
def low_back(v):
    return v

def low_keep(v):
    return (low(v), None)

def low_pass(kept, grad):
    return (grad,)

def back_keep(v):
    return (v, None)

def back_low(kept, grad):
    return (low(grad),)
low.defvjp(low_keep, low_pass)
low_back.defvjp(back_keep, back_low)
epsilon = 1e-05

def product(form, left, right):
    return jnp.einsum(form, left, right, precision=lax.Precision.HIGHEST, preferred_element_type=jnp.float32)

def normalize(values):
    center = values - lax.optimization_barrier(jnp.mean(values, -1, keepdims=True))
    spread = lax.optimization_barrier(jnp.mean(center * center, -1, keepdims=True))
    return center * lax.rsqrt(spread + epsilon)

def rotary(count, head):
    half = head // 2
    freqs = 10000.0 ** (-2.0 * jnp.arange(half, dtype=jnp.float32) / head)
    angles = jnp.arange(count, dtype=jnp.float32)[:, None] * freqs[None, :]
    cosine = jnp.concatenate([jnp.cos(angles), jnp.cos(angles)], -1)
    sine = jnp.concatenate([jnp.sin(angles), jnp.sin(angles)], -1)
    return (cosine, sine)

def rotate(values, cosine, sine):
    half = values.shape[-1] // 2
    turned = jnp.concatenate([-values[..., half:], values[..., :half]], -1)
    return values * cosine[:, None, :] + turned * sine[:, None, :]

def attend(queries, keys, values):
    scores = low_back(product('qhd,khd->hqk', queries, keys) * HD ** (-0.5))
    probs = jax.nn.softmax(scores, axis=-1)
    return product('hqk,khd->qhd', probs, values)

def forward(tokens, time_table, ada_weight, ada_bias, attn_gain, qkv_weight, out_weight, mlp_gain, up_weight, up_bias, down_weight, down_bias, mask_vector, time_index, absorbed):
    cond = jax.nn.silu(time_table[time_index])
    modulation = product('bc,ce->be', cond, ada_weight) + ada_bias
    parts = [modulation[:, None, piece * D:(piece + 1) * D] for piece in range(6)]
    shift_attn, scale_attn, gate_attn, shift_mlp, scale_mlp, gate_mlp = parts
    start = jnp.where(absorbed[..., None] == 1, mask_vector, tokens)
    mixed_attn = low(normalize(start) * attn_gain * (1.0 + scale_attn) + shift_attn)
    qkv = low_back(product('btd,de->bte', mixed_attn, qkv_weight))
    cosine, sine = rotary(SEQ, HD)
    block = math.gcd(SEQ, 512)
    checked = jax.checkpoint(attend)
    results = []
    for sequence in range(B):
        query = low(rotate(qkv[sequence, :, :D].reshape(SEQ, H, HD), cosine, sine))
        keys = low(rotate(qkv[sequence, :, D:2 * D].reshape(SEQ, H, HD), cosine, sine))
        values = low(qkv[sequence, :, 2 * D:].reshape(SEQ, H, HD))
        blocks = query.reshape(SEQ // block, block, H, HD)
        done = lax.map(lambda query_block: checked(query_block, keys, values), blocks)
        results.append(done.reshape(SEQ, D))
    attended = jnp.stack(results)
    used = low(low_back(attended))
    attn = low_back(product('btd,de->bte', used, out_weight))
    middle = start + gate_attn * attn
    mixed_mlp = low(normalize(middle) * mlp_gain * (1.0 + scale_mlp) + shift_mlp)
    upper = low_back(product('btd,df->btf', mixed_mlp, up_weight) + up_bias)
    hidden = low(jax.nn.gelu(upper, approximate=True))
    lowered = low_back(product('btf,fd->btd', hidden, down_weight) + down_bias)
    return middle + gate_mlp * lowered

def reference(tokens, cotangent, time_index, absorbed, time_table, ada_weight, ada_bias, attn_gain, qkv_weight, out_weight, mlp_gain, up_weight, up_bias, down_weight, down_bias, mask_vector):
    floats = [array.astype(jnp.float32) for array in (tokens, time_table, ada_weight, ada_bias, attn_gain, qkv_weight, out_weight, mlp_gain, up_weight, up_bias, down_weight, down_bias, mask_vector)]

    def run(*arrays):
        return forward(*arrays, time_index, absorbed)
    output, pull = jax.vjp(run, *floats)
    grads = pull(cotangent.astype(jnp.float32))
    return (output, grads[0], grads[1], grads[2], grads[3], grads[4], grads[5], grads[6], grads[7], grads[8], grads[9], grads[10], grads[11], grads[12])
```

```python
import functools

import jax
import jax.numpy as jnp
from jax import lax
from jax.experimental import pallas as pl
from jax.experimental.pallas import tpu as pltpu
from jax.sharding import PartitionSpec as P

H = 12


epsilon = 1e-05
precise = lax.Precision.HIGHEST
lowest = -1e30


def shifted(value, axis, steps):
    count = lax.axis_size(axis)
    pairs = [(source, (source + steps) % count) for source in range(count)]
    return lax.ppermute(value, axis, pairs)


def combined_all(value, axis, join):
    pieces = jax.tree.map(lambda part: lax.all_gather(part, axis), value)
    head = jax.tree.map(lambda part: part[0], pieces)
    tail = jax.tree.map(lambda part: part[1:], pieces)
    subtotal, _ = lax.scan(lambda subtotal, slab: (join(subtotal, slab), None), head, tail)
    return subtotal


def to_half(values):
    return values.astype(jnp.bfloat16)


def normalize(values):
    center = values - jnp.mean(values, -1, keepdims=True)
    spread = jnp.mean(center * center, -1, keepdims=True)
    return center * lax.rsqrt(spread + epsilon)


def premix(values, gain, shift, scale):
    return normalize(values) * gain * (1.0 + scale) + shift


def rotary(positions, head):
    half = head // 2
    freqs = 10000.0 ** (-2.0 * jnp.arange(half, dtype=jnp.float32) / head)
    angles = positions[:, None] * freqs[None, :]
    cosine = jnp.concatenate([jnp.cos(angles), jnp.cos(angles)], -1)
    sine = jnp.concatenate([jnp.sin(angles), jnp.sin(angles)], -1)
    return (cosine, sine)


def turn_half(values):
    half = values.shape[-1] // 2
    return jnp.concatenate([-values[..., half:], values[..., :half]], -1)


def rotate(values, cosine, sine, direction):
    return (
        values * cosine[None, :, None, :] + direction * turn_half(values) * sine[None, :, None, :]
    )


def fetch_attn(time_table, ada_weight, ada_bias, attn_gain, qkv_weight, out_weight, mask_vector):
    return (
        lax.all_gather(time_table, "fsdp", axis=0, tiled=True),
        lax.all_gather(ada_weight, "fsdp", axis=0, tiled=True),
        lax.all_gather(ada_bias, "fsdp", axis=0, tiled=True),
        lax.all_gather(attn_gain, "fsdp", axis=0, tiled=True),
        lax.all_gather(qkv_weight, "fsdp", axis=0, tiled=True),
        lax.all_gather(out_weight, "fsdp", axis=0, tiled=True),
        lax.all_gather(mask_vector, "fsdp", axis=0, tiled=True),
    )


def fetch_mlp(mlp_gain, up_weight, up_bias, down_weight, down_bias):
    return (
        lax.all_gather(mlp_gain, "fsdp", axis=0, tiled=True),
        lax.all_gather(up_weight, "fsdp", axis=0, tiled=True),
        lax.all_gather(up_bias, "fsdp", axis=0, tiled=True),
        lax.all_gather(down_weight, "fsdp", axis=0, tiled=True),
        lax.all_gather(down_bias, "fsdp", axis=0, tiled=True),
    )


def online(carry, keys, values, query4):
    best, total, summed = carry
    batch, count, heads, head = query4.shape
    key4 = keys.reshape(batch, -1, heads, head)
    value4 = values.reshape(batch, -1, heads, head)
    scores = jnp.einsum(
        "bqhd,bkhd->bqhk", query4, key4, preferred_element_type=jnp.float32
    ) * head ** (-0.5)
    raised = jnp.maximum(best, jnp.max(scores, -1))
    factor = jnp.exp(best - raised)
    weights = jnp.exp(scores - raised[..., None])
    total = total * factor + jnp.sum(weights, -1)
    update = jnp.einsum("bqhk,bkhd->bqhd", weights, value4, preferred_element_type=jnp.float32)
    summed = summed.reshape(batch, count, heads, head) * factor[..., None] + update
    return (raised, total, summed.reshape(batch, count, heads * head))


def fold_keys(carry, piece, query4):
    keys, values = piece
    count = keys.shape[1]
    splits = 1
    while count // splits > 256 and count % (splits * 2) == 0:
        splits = splits * 2
    batch = keys.shape[0]
    width = keys.shape[2]
    key_blocks = jnp.moveaxis(keys.reshape(batch, splits, count // splits, width), 1, 0)
    value_blocks = jnp.moveaxis(values.reshape(batch, splits, count // splits, width), 1, 0)

    def advance(state, pair):
        return (online(state, pair[0], pair[1], query4), None)

    carry, unused = lax.scan(advance, carry, (key_blocks, value_blocks))
    return carry


def combine(first, second):
    raised = jnp.maximum(first[0], second[0])
    left = jnp.exp(first[0] - raised)
    right = jnp.exp(second[0] - raised)
    batch, count, heads = raised.shape
    total = first[1] * left + second[1] * right
    summed = (
        first[2].reshape(batch, count, heads, -1) * left[..., None]
        + second[2].reshape(batch, count, heads, -1) * right[..., None]
    )
    return (raised, total, summed.reshape(batch, count, -1))


def block_grads(keys, values, query4, grad4, logsum, delta):
    batch, count, heads, head = query4.shape
    key4 = keys.reshape(batch, -1, heads, head)
    value4 = values.reshape(batch, -1, heads, head)
    factor = head ** (-0.5)
    scores = (
        jnp.einsum("bqhd,bkhd->bqhk", query4, key4, preferred_element_type=jnp.float32) * factor
    )
    probs = jnp.exp(scores - logsum[..., None])
    grad_probs = jnp.einsum("bqhd,bkhd->bqhk", grad4, value4, preferred_element_type=jnp.float32)
    grad_scores = to_half(probs * (grad_probs - delta[..., None]))
    query_add = (
        jnp.einsum("bqhk,bkhd->bqhd", grad_scores, key4, preferred_element_type=jnp.float32)
        * factor
    )
    key_add = (
        jnp.einsum("bqhk,bqhd->bkhd", grad_scores, query4, preferred_element_type=jnp.float32)
        * factor
    )
    value_add = jnp.einsum("bqhk,bqhd->bkhd", probs, grad4, preferred_element_type=jnp.float32)
    return (
        query_add.reshape(batch, count, -1),
        key_add.reshape(keys.shape),
        value_add.reshape(values.shape),
    )


def pass_keys(keys, values):
    return shifted((keys, values), "ctx", 1)


def pass_grads(key_grad, value_grad):
    return (
        shifted(key_grad.astype(jnp.bfloat16), "ctx", 1).astype(key_grad.dtype),
        shifted(value_grad.astype(jnp.bfloat16), "ctx", 1).astype(value_grad.dtype),
    )


def ring_shards(
    tokens,
    cotangent,
    time_index,
    absorbed,
    time_table,
    ada_weight,
    ada_bias,
    attn_gain,
    qkv_weight,
    out_weight,
    mlp_gain,
    up_weight,
    up_bias,
    down_weight,
    down_bias,
    mask_vector,
):
    batch, rows, width = tokens.shape
    heads = H
    head = width // heads
    fsdp_count = lax.axis_size("fsdp")
    cycle_count = lax.axis_size("ctx")
    stop_place = lax.axis_index("fsdp")
    device_place = lax.axis_index("ctx") * fsdp_count + stop_place
    table_full, ada_full, ada_bias_full, attn_gain_full, qkv_full, out_full, mask_full = fetch_attn(
        time_table, ada_weight, ada_bias, attn_gain, qkv_weight, out_weight, mask_vector
    )
    steps_total = table_full.shape[0]
    onehot = (time_index[:, None] == jnp.arange(steps_total, dtype=jnp.int32)[None, :]).astype(
        jnp.float32
    )
    raw_time = jnp.dot(onehot, table_full.astype(jnp.float32), precision=precise)
    cond, silu_pull = jax.vjp(jax.nn.silu, raw_time)
    modulation = jnp.dot(
        cond, ada_full.astype(jnp.float32), precision=precise
    ) + ada_bias_full.astype(jnp.float32)
    pieces = [modulation[:, None, part * width : (part + 1) * width] for part in range(6)]
    shift_attn, scale_attn, gate_attn, shift_mlp, scale_mlp, gate_mlp = pieces
    masked = (absorbed == 1)[..., None]
    start = jnp.where(masked, mask_full.astype(jnp.float32), tokens.astype(jnp.float32))
    attn_gain_wide = attn_gain_full.astype(jnp.float32)
    mixed_attn = to_half(premix(start, attn_gain_wide, shift_attn, scale_attn))
    qkv = jnp.einsum("btd,de->bte", mixed_attn, qkv_full, preferred_element_type=jnp.float32)
    positions = (device_place * rows + jnp.arange(rows, dtype=jnp.int32)).astype(jnp.float32)
    cosine, sine = rotary(positions, head)
    query_own = to_half(
        rotate(qkv[..., :width].reshape(batch, rows, heads, head), cosine, sine, 1.0)
    ).reshape(batch, rows, width)
    key_own = to_half(
        rotate(qkv[..., width : 2 * width].reshape(batch, rows, heads, head), cosine, sine, 1.0)
    ).reshape(batch, rows, width)
    value_own = to_half(qkv[..., 2 * width :])
    query_stop = lax.all_gather(query_own, "fsdp", axis=1, tiled=True)
    stop_rows = query_stop.shape[1]
    query4 = query_stop.reshape(batch, stop_rows, heads, head)
    start_state = (
        jnp.full((batch, stop_rows, heads), lowest, jnp.float32),
        jnp.zeros((batch, stop_rows, heads), jnp.float32),
        jnp.zeros((batch, stop_rows, width), jnp.float32),
    )
    best, total, summed = fold_keys(
        start_state,
        (
            lax.all_gather(key_own, "ctx", axis=1, tiled=True),
            lax.all_gather(value_own, "ctx", axis=1, tiled=True),
        ),
        query4,
    )
    best, total, summed = combined_all((best, total, summed), "fsdp", combine)
    logsum = best + jnp.log(total)
    attended_stop = (summed.reshape(batch, stop_rows, heads, head) / total[..., None]).reshape(
        batch, stop_rows, width
    )
    attended = lax.dynamic_slice_in_dim(attended_stop, stop_place * rows, rows, 1)
    attended_low = to_half(attended)
    attn = jnp.einsum("btd,de->bte", attended_low, out_full, preferred_element_type=jnp.float32)
    middle = start + gate_attn * attn
    mlp_gain_full, up_full, up_bias_full, down_full, down_bias_full = fetch_mlp(
        mlp_gain, up_weight, up_bias, down_weight, down_bias
    )
    mlp_gain_wide = mlp_gain_full.astype(jnp.float32)
    mixed_mlp = to_half(premix(middle, mlp_gain_wide, shift_mlp, scale_mlp))
    upper = jnp.einsum(
        "btd,df->btf", mixed_mlp, up_full, preferred_element_type=jnp.float32
    ) + up_bias_full.astype(jnp.float32)
    hidden = to_half(jax.nn.gelu(upper, approximate=True))
    lowered = jnp.einsum(
        "btf,fd->btd", hidden, down_full, preferred_element_type=jnp.float32
    ) + down_bias_full.astype(jnp.float32)
    output = middle + gate_mlp * lowered
    mlp_gain_full, up_full, up_bias_full, down_full, down_bias_full = fetch_mlp(
        mlp_gain, up_weight, up_bias, down_weight, down_bias
    )
    grad_out = cotangent.astype(jnp.float32)
    grad_lowered = to_half(grad_out * gate_mlp)
    grad_gate_mlp = jnp.sum(grad_out * lowered, 1)
    grad_down_bias = jnp.sum(grad_lowered.astype(jnp.float32), (0, 1))
    grad_down_weight = jnp.einsum(
        "btf,btd->fd", hidden, grad_lowered, preferred_element_type=jnp.float32
    )
    grad_hidden = jnp.einsum(
        "btd,fd->btf", grad_lowered, down_full, preferred_element_type=jnp.float32
    )
    gelu_pull = jax.vjp(lambda values: jax.nn.gelu(values, approximate=True), upper)[1]
    grad_upper = to_half(gelu_pull(grad_hidden)[0])
    grad_up_bias = jnp.sum(grad_upper.astype(jnp.float32), (0, 1))
    grad_up_weight = jnp.einsum(
        "btd,btf->df", mixed_mlp, grad_upper, preferred_element_type=jnp.float32
    )
    grad_mixed_mlp = jnp.einsum(
        "btf,df->btd", grad_upper, up_full, preferred_element_type=jnp.float32
    )
    mlp_pull = jax.vjp(premix, middle, mlp_gain_wide, shift_mlp, scale_mlp)[1]
    grad_middle_part, grad_mlp_gain, grad_shift_mlp, grad_scale_mlp = mlp_pull(grad_mixed_mlp)
    grad_middle = grad_out + grad_middle_part
    table_full, ada_full, ada_bias_full, attn_gain_full, qkv_full, out_full, mask_full = fetch_attn(
        time_table, ada_weight, ada_bias, attn_gain, qkv_weight, out_weight, mask_vector
    )
    grad_attn = to_half(grad_middle * gate_attn)
    grad_gate_attn = jnp.sum(grad_middle * attn, 1)
    grad_out_weight = jnp.einsum(
        "btd,bte->de", attended_low, grad_attn, preferred_element_type=jnp.float32
    )
    grad_attended = to_half(
        jnp.einsum("bte,de->btd", grad_attn, out_full, preferred_element_type=jnp.float32)
    )
    grad_stop = lax.all_gather(grad_attended, "fsdp", axis=1, tiled=True)
    grad4 = grad_stop.reshape(batch, stop_rows, heads, head)
    delta = jnp.sum(
        grad4.astype(jnp.float32) * attended_stop.reshape(batch, stop_rows, heads, head), -1
    )
    zeros_stop = jnp.zeros((batch, stop_rows, width), jnp.float32)

    def cycle_turn(position, state):
        keys, values, key_grad, value_grad, query_grad = state
        query_add, key_add, value_add = block_grads(keys, values, query4, grad4, logsum, delta)
        keys, values = pass_keys(keys, values)
        key_grad, value_grad = pass_grads(key_grad + key_add, value_grad + value_add)
        return (keys, values, key_grad, value_grad, query_grad + query_add)

    zeros_own = jnp.zeros((batch, rows, width), jnp.float32)
    keys, values, key_grad, value_grad, query_sum = lax.fori_loop(
        0, cycle_count - 1, cycle_turn, (key_own, value_own, zeros_own, zeros_own, zeros_stop)
    )
    query_add, key_add, value_add = block_grads(keys, values, query4, grad4, logsum, delta)
    key_grad, value_grad = pass_grads(key_grad + key_add, value_grad + value_add)
    query_partial = query_sum + query_add
    query_grad = lax.psum_scatter(
        query_partial.astype(jnp.bfloat16), "fsdp", scatter_dimension=1, tiled=True
    ).astype(jnp.float32)
    grad_query = rotate(query_grad.reshape(batch, rows, heads, head), cosine, sine, -1.0).reshape(
        batch, rows, width
    )
    grad_key = rotate(key_grad.reshape(batch, rows, heads, head), cosine, sine, -1.0).reshape(
        batch, rows, width
    )
    grad_qkv = to_half(jnp.concatenate([grad_query, grad_key, value_grad], -1))
    grad_qkv_weight = jnp.einsum(
        "btd,bte->de", mixed_attn, grad_qkv, preferred_element_type=jnp.float32
    )
    grad_mixed_attn = jnp.einsum(
        "bte,de->btd", grad_qkv, qkv_full, preferred_element_type=jnp.float32
    )
    attn_pull = jax.vjp(premix, start, attn_gain_wide, shift_attn, scale_attn)[1]
    grad_start_part, grad_attn_gain, grad_shift_attn, grad_scale_attn = attn_pull(grad_mixed_attn)
    grad_start = grad_middle + grad_start_part
    grad_tokens = jnp.where(masked, 0.0, grad_start)
    grad_mask_vector = jnp.sum(jnp.where(masked, grad_start, 0.0), (0, 1))
    grad_modulation = jnp.concatenate(
        [
            grad_shift_attn[:, 0],
            grad_scale_attn[:, 0],
            grad_gate_attn,
            grad_shift_mlp[:, 0],
            grad_scale_mlp[:, 0],
            grad_gate_mlp,
        ],
        -1,
    )
    grad_ada_bias = jnp.sum(grad_modulation, 0)
    grad_ada_weight = jnp.dot(cond.T, grad_modulation, precision=precise)
    grad_cond = jnp.dot(grad_modulation, ada_full.astype(jnp.float32).T, precision=precise)
    grad_raw = silu_pull(grad_cond)[0]
    grad_table = jnp.dot(onehot.T, grad_raw, precision=precise)
    summed_grads = (
        lax.psum_scatter(grad_table, ("ctx", "fsdp"), scatter_dimension=0, tiled=True),
        lax.psum_scatter(grad_ada_weight, ("ctx", "fsdp"), scatter_dimension=0, tiled=True),
        lax.psum_scatter(grad_ada_bias, ("ctx", "fsdp"), scatter_dimension=0, tiled=True),
        lax.psum_scatter(grad_attn_gain, ("ctx", "fsdp"), scatter_dimension=0, tiled=True),
        lax.psum_scatter(grad_qkv_weight, ("ctx", "fsdp"), scatter_dimension=0, tiled=True),
        lax.psum_scatter(grad_out_weight, ("ctx", "fsdp"), scatter_dimension=0, tiled=True),
        lax.psum_scatter(grad_mlp_gain, ("ctx", "fsdp"), scatter_dimension=0, tiled=True),
        lax.psum_scatter(grad_up_weight, ("ctx", "fsdp"), scatter_dimension=0, tiled=True),
        lax.psum_scatter(grad_up_bias, ("ctx", "fsdp"), scatter_dimension=0, tiled=True),
        lax.psum_scatter(grad_down_weight, ("ctx", "fsdp"), scatter_dimension=0, tiled=True),
        lax.psum_scatter(grad_down_bias, ("ctx", "fsdp"), scatter_dimension=0, tiled=True),
        lax.psum_scatter(grad_mask_vector, ("ctx", "fsdp"), scatter_dimension=0, tiled=True),
    )
    (
        grad_table,
        grad_ada_weight,
        grad_ada_bias,
        grad_attn_gain,
        grad_qkv_weight,
        grad_out_weight,
        grad_mlp_gain,
        grad_up_weight,
        grad_up_bias,
        grad_down_weight,
        grad_down_bias,
        grad_mask_vector,
    ) = summed_grads
    return (
        output,
        grad_tokens,
        grad_table,
        grad_ada_weight,
        grad_ada_bias,
        grad_attn_gain,
        grad_qkv_weight,
        grad_out_weight,
        grad_mlp_gain,
        grad_up_weight,
        grad_up_bias,
        grad_down_weight,
        grad_down_bias,
        grad_mask_vector,
    )

outlier = 1e30
pair_form = (((1,), (1,)), ((), ()))
plain_form = (((1,), (0,)), ((), ()))
slim_form = (((0,), (0,)), ((), ()))
curve = 0.7978845608028654
cube = 0.044715


def product(left, right, form=plain_form):
    return lax.dot_general(left, right, form, preferred_element_type=jnp.float32)


def mirrored(value, axis, flip):
    count = lax.axis_size(axis)
    return lax.ppermute(value, axis, [(place, place ^ flip) for place in range(count)])


def picked(value, place, axis=0):
    return lax.dynamic_index_in_dim(value, place, axis, keepdims=False)


def whole(shape):
    return pl.BlockSpec(shape, lambda *_: (0,) * len(shape))


def params(count=1):
    return pltpu.CompilerParams(
        vmem_limit_bytes=50 * 1024 * 1024, dimension_semantics=("arbitrary",) * count
    )


def half_turn(values):
    lane = lax.broadcasted_iota(jnp.int32, values.shape, 1)
    span = values.shape[1]
    return jnp.where(
        lane < span // 4,
        pltpu.roll(values, span - span // 4, 1),
        pltpu.roll(values, span // 4, 1),
    )


def centered(values):
    center = values - jnp.mean(values, -1, keepdims=True)
    spread = jnp.mean(center * center, -1, keepdims=True)
    scale = lax.rsqrt(spread + epsilon)
    return center * scale, scale


def started(coded, mask_row):
    return jnp.where(coded > 1e29, mask_row, coded)


def entry_kernel(coded_ref, vec_ref, weight_ref, cos_ref, sin_ref, mixed_ref, kv_ref, query_ref):
    start = started(coded_ref[...].astype(jnp.float32), vec_ref[0:1, :])
    normed, _ = centered(start)
    mixed = to_half(normed * vec_ref[1:2, :] * (1.0 + vec_ref[2:3, :]) + vec_ref[3:4, :])
    mixed_ref[...] = mixed
    both = product(mixed, weight_ref[...])
    cosine, sine = cos_ref[...], sin_ref[...]
    span = cosine.shape[1]
    groups = both.shape[1] // span
    half = groups // 2
    factor = (span // 2) ** (-0.5)
    for place in range(groups):
        values = both[:, place * span : (place + 1) * span]
        turned = to_half(values * cosine + half_turn(values) * sine)
        if place < half:
            kv_ref[:, place * span : (place + 1) * span] = turned
        else:
            query_ref[:, (place - half) * span : (place - half + 1) * span] = turned * to_half(
                jnp.float32(factor)
            )


def entry(coded, vectors, weight, cosine, sine, block):
    count, width = coded.shape
    span = cosine.shape[1]
    wide = weight.shape[1] // 2
    row = pl.BlockSpec((block, width), lambda step: (step, 0))
    table = pl.BlockSpec((block, span), lambda step: (step, 0))
    piece = pl.BlockSpec((block, wide), lambda step: (step, 0))
    return pl.pallas_call(
        entry_kernel,
        grid=(count // block,),
        in_specs=[row, whole(vectors.shape), whole(weight.shape), table, table],
        out_specs=[row, piece, piece],
        out_shape=[
            jax.ShapeDtypeStruct((count, width), jnp.bfloat16),
            jax.ShapeDtypeStruct((count, wide), jnp.bfloat16),
            jax.ShapeDtypeStruct((count, wide), jnp.bfloat16),
        ],
        compiler_params=params(),
        cost_estimate=pl.CostEstimate(
            flops=2 * count * width * wide * 2, bytes_accessed=8 * count * width, transcendentals=0
        ),
        name="entry",
    )(coded, vectors, weight, cosine, sine)


def attend_kernel(query_ref, near_ref, far_ref, out_ref, exp_ref, inv_ref, turned, scores, *, chunk):
    count, span = near_ref.shape
    half = span // 2

    @pl.when(pl.program_id(1) == 0)
    def _():
        row = lax.broadcasted_iota(jnp.int32, (span, count), 0)
        for place, ref in enumerate((near_ref, far_ref)):
            flat = ref[...].astype(jnp.float32).T
            turned[:, place * count : (place + 1) * count] = to_half(jnp.where(row < half, 1.0, flat))

    query = query_ref[...]
    best = None
    pieces = count // chunk
    for place in range(2 * pieces):
        ref = (near_ref, far_ref)[place // pieces]
        low = (place % pieces) * chunk
        part = product(ref[low : low + chunk, :], query, pair_form)
        scores[place * chunk : (place + 1) * chunk, :] = part
        top = jnp.max(part, axis=0, keepdims=True)
        best = top if best is None else jnp.maximum(best, top)
    total = None
    for place in range(2 * pieces):
        part = to_half(jnp.exp(scores[place * chunk : (place + 1) * chunk, :] - best))
        exp_ref[0, place * chunk : (place + 1) * chunk, :] = part
        add = product(turned[:, place * chunk : (place + 1) * chunk], part)
        total = add if total is None else total + add
    inverse = 1.0 / total[0:1, :]
    out_ref[...] = to_half(total[half:, :] * inverse)
    inv_ref[0] = inverse


def attend(query, near, far, span, block, chunk):
    count = query.shape[0]
    heads = query.shape[1] // span
    keys = near.shape[0]
    stay = pl.BlockSpec((keys, span), lambda head, step: (0, head))
    return pl.pallas_call(
        functools.partial(attend_kernel, chunk=chunk),
        grid=(heads, count // block),
        in_specs=[pl.BlockSpec((block, span), lambda head, step: (step, head)), stay, stay],
        out_specs=[
            pl.BlockSpec((span // 2, block), lambda head, step: (head, step)),
            pl.BlockSpec((1, 2 * keys, block), lambda head, step: (head, 0, step)),
            pl.BlockSpec((1, 1, block), lambda head, step: (head, 0, step)),
        ],
        out_shape=[
            jax.ShapeDtypeStruct((heads * span // 2, count), jnp.bfloat16),
            jax.ShapeDtypeStruct((heads, 2 * keys, count), jnp.bfloat16),
            jax.ShapeDtypeStruct((heads, 1, count), jnp.float32),
        ],
        scratch_shapes=[
            pltpu.VMEM((span, 2 * keys), jnp.bfloat16),
            pltpu.VMEM((2 * keys, block), jnp.float32),
        ],
        compiler_params=params(2),
        cost_estimate=pl.CostEstimate(
            flops=8 * heads * count * keys * span,
            bytes_accessed=4 * heads * count * keys,
            transcendentals=2 * heads * count * keys,
        ),
        name="attend",
    )(query, near, far)


def attend_back_kernel(
    query_ref, grad_ref, out_ref, exp_ref, inv_ref, near_ref, far_ref,
    query_grad_ref, near_grad_ref, far_grad_ref, turned, sums, *, chunk
):
    count, span = near_ref.shape
    half = span // 2
    step = pl.program_id(1)

    @pl.when(step == 0)
    def _():
        for place, ref in enumerate((near_ref, far_ref)):
            flat = ref[...].astype(jnp.float32).T
            turned[:, place * count : (place + 1) * count] = to_half(flat)[:half]
        sums[...] = jnp.zeros_like(sums)

    inverse = inv_ref[0]
    grad = grad_ref[...].astype(jnp.float32) * inverse
    delta = jnp.sum(grad * out_ref[...].astype(jnp.float32), axis=0, keepdims=True)
    padded = jnp.concatenate([jnp.zeros_like(grad), grad], 0)
    side = to_half(padded)
    upright = to_half(padded.T)
    query = query_ref[...]
    pieces = count // chunk
    total = None
    for place in range(2 * pieces):
        ref = (near_ref, far_ref)[place // pieces]
        low = (place % pieces) * chunk
        part = product(ref[low : low + chunk, :], side)
        weights = exp_ref[0, place * chunk : (place + 1) * chunk, :]
        grad_scores = to_half(weights.astype(jnp.float32) * (part - delta))
        sums[place * chunk : (place + 1) * chunk, :] += product(grad_scores, query) + product(
            weights, upright
        )
        add = product(turned[:, place * chunk : (place + 1) * chunk], grad_scores)
        total = add if total is None else total + add
    total = total * (half ** (-0.5))
    query_grad_ref[...] = jnp.concatenate([total, jnp.zeros_like(total)], 0).T

    @pl.when(step == pl.num_programs(1) - 1)
    def _():
        near_grad_ref[...] = sums[:count, :]
        far_grad_ref[...] = to_half(sums[count:, :])


def attend_back(query, grad, out, weights, inverse, near, far, span, block, chunk):
    count = query.shape[0]
    heads = query.shape[1] // span
    keys = near.shape[0]
    stay = pl.BlockSpec((keys, span), lambda head, step: (0, head))
    flow = pl.BlockSpec((block, span), lambda head, step: (step, head))
    flat = pl.BlockSpec((span // 2, block), lambda head, step: (head, step))
    return pl.pallas_call(
        functools.partial(attend_back_kernel, chunk=chunk),
        grid=(heads, count // block),
        in_specs=[
            flow,
            flat,
            flat,
            pl.BlockSpec((1, 2 * keys, block), lambda head, step: (head, 0, step)),
            pl.BlockSpec((1, 1, block), lambda head, step: (head, 0, step)),
            stay,
            stay,
        ],
        out_specs=[flow, stay, stay],
        out_shape=[
            jax.ShapeDtypeStruct((count, heads * span), jnp.float32),
            jax.ShapeDtypeStruct((keys, heads * span), jnp.float32),
            jax.ShapeDtypeStruct((keys, heads * span), jnp.bfloat16),
        ],
        scratch_shapes=[
            pltpu.VMEM((span // 2, 2 * keys), jnp.bfloat16),
            pltpu.VMEM((2 * keys, span), jnp.float32),
        ],
        compiler_params=params(2),
        cost_estimate=pl.CostEstimate(
            flops=16 * heads * count * keys * span,
            bytes_accessed=4 * heads * count * keys,
            transcendentals=0,
        ),
        name="attend_back",
    )(query, grad, out, weights, inverse, near, far)


def middle_kernel(
    first_ref, second_ref, third_ref, fourth_ref, coded_ref, cot_ref, vec_ref, bias_ref,
    out_weight_ref, up_ref, down_ref,
    back_ref, hidden_ref, mixed_ref, upper_grad_ref, lowered_grad_ref, attn_ref, bias_grad_ref
):
    step = pl.program_id(0)
    start = started(coded_ref[...].astype(jnp.float32), vec_ref[0:1, :])
    sideways = jnp.concatenate(
        [first_ref[...], second_ref[...], third_ref[...], fourth_ref[...]], 0
    )
    attn = product(sideways, out_weight_ref[...], slim_form)

    @pl.when(step == 0)
    def _():
        attn_ref[...] = attn
        bias_grad_ref[...] = jnp.zeros_like(bias_grad_ref)

    middle = start + vec_ref[4:5, :] * attn
    normed, _ = centered(middle)
    mixed = to_half(normed * vec_ref[5:6, :] * (1.0 + vec_ref[6:7, :]) + vec_ref[7:8, :])
    mixed_ref[...] = mixed
    upper = product(mixed, up_ref[...]) + bias_ref[...]
    square = upper * upper
    level = jnp.tanh(curve * upper * (1.0 + cube * square))
    hidden_ref[...] = to_half(0.5 * upper * (1.0 + level))
    slope = 0.5 * (1.0 + level) + (0.5 * curve) * upper * (1.0 - level * level) * (
        1.0 + (3.0 * cube) * square
    )
    lowered_grad = to_half(cot_ref[...].astype(jnp.float32) * vec_ref[8:9, :])
    lowered_grad_ref[...] = lowered_grad
    upper_grad = to_half(product(lowered_grad, down_ref[...], pair_form) * slope)
    upper_grad_ref[...] = upper_grad
    bias_grad_ref[0:1, :] += jnp.sum(upper_grad.astype(jnp.float32), 0, keepdims=True)
    back_ref[...] = to_half(product(upper_grad, up_ref[...], pair_form))


def middle_stage(outs, coded, cot, vectors, bias, out_weight, up, down, block):
    count, width = coded.shape
    hidden = up.shape[1]
    row = pl.BlockSpec((block, width), lambda step: (step, 0))
    high = pl.BlockSpec((block, hidden), lambda step: (step, 0))
    lanes = outs[0].shape[0]
    sides = [
        pl.BlockSpec((lanes, block), functools.partial(lambda flip, step: (0, step ^ flip), flip))
        for flip in range(4)
    ]
    half = jnp.bfloat16
    return pl.pallas_call(
        middle_kernel,
        grid=(count // block,),
        in_specs=sides
        + [row, row, whole(vectors.shape), whole(bias.shape)]
        + [whole(out_weight.shape), whole(up.shape), whole(down.shape)],
        out_specs=[row, high, row, high, row, whole((block, width)), whole((8, hidden))],
        out_shape=[
            jax.ShapeDtypeStruct((count, width), half),
            jax.ShapeDtypeStruct((count, hidden), half),
            jax.ShapeDtypeStruct((count, width), half),
            jax.ShapeDtypeStruct((count, hidden), half),
            jax.ShapeDtypeStruct((count, width), half),
            jax.ShapeDtypeStruct((block, width), jnp.float32),
            jax.ShapeDtypeStruct((8, hidden), jnp.float32),
        ],
        compiler_params=params(),
        cost_estimate=pl.CostEstimate(
            flops=2 * count * width * (width + 3 * hidden),
            bytes_accessed=16 * count * width,
            transcendentals=count * hidden,
        ),
        name="middle",
    )(*outs, coded, cot, vectors, bias, out_weight, up, down)


def turn_kernel(
    own_ref, second_ref, third_ref, fourth_ref, coded_ref, cot_ref, attn_ref, vec_ref, out_weight_ref,
    middle_grad_ref, attn_grad_ref, side_ref, sums_ref
):
    coded = coded_ref[...].astype(jnp.float32)
    start = started(coded, vec_ref[0:1, :])
    attn = attn_ref[...]
    middle = start + vec_ref[4:5, :] * attn
    normed, scale = centered(middle)
    grad = (
        own_ref[...].astype(jnp.float32)
        + second_ref[...].astype(jnp.float32)
        + third_ref[...].astype(jnp.float32)
        + fourth_ref[...].astype(jnp.float32)
    )
    swell = grad * (1.0 + vec_ref[6:7, :]) * vec_ref[5:6, :]
    level = jnp.mean(swell, -1, keepdims=True)
    slope = jnp.mean(swell * normed, -1, keepdims=True)
    middle_grad = cot_ref[...].astype(jnp.float32) + scale * (swell - level - normed * slope)
    middle_grad_ref[...] = middle_grad
    attn_grad = to_half(middle_grad * vec_ref[4:5, :])
    attn_grad_ref[...] = attn_grad
    side_ref[...] = to_half(product(out_weight_ref[...], attn_grad, pair_form))
    sums_ref[...] = jnp.concatenate(
        [
            jnp.sum(grad, 0, keepdims=True),
            jnp.sum(grad * normed, 0, keepdims=True),
            jnp.sum(middle_grad * attn, 0, keepdims=True),
            jnp.sum(jnp.where(coded > 1e29, middle_grad, 0.0), 0, keepdims=True),
            jnp.zeros((4, grad.shape[1]), jnp.float32),
        ],
        0,
    )


def turn_stage(backs, coded, cot, attn, vectors, out_weight):
    count, width = attn.shape
    row = whole((count, width))
    return pl.pallas_call(
        turn_kernel,
        grid=(1,),
        in_specs=[row] * 7 + [whole(vectors.shape), whole(out_weight.shape)],
        out_specs=[row, row, whole((width, count)), whole((8, width))],
        out_shape=[
            jax.ShapeDtypeStruct((count, width), jnp.float32),
            jax.ShapeDtypeStruct((count, width), jnp.bfloat16),
            jax.ShapeDtypeStruct((width, count), jnp.bfloat16),
            jax.ShapeDtypeStruct((8, width), jnp.float32),
        ],
        compiler_params=params(),
        cost_estimate=pl.CostEstimate(
            flops=2 * count * width * width, bytes_accessed=16 * count * width, transcendentals=0
        ),
        name="turn",
    )(*backs, coded, cot, attn, vectors, out_weight)


def exit_kernel(
    query_ref, near_ref, far_ref, cos_ref, sin_ref, coded_ref, vec_ref, weight_ref,
    start_grad_ref, packed_ref, sums_ref
):
    step = pl.program_id(0)
    cosine, sine = cos_ref[...], sin_ref[...]
    span = cosine.shape[1]
    wide = near_ref.shape[1]
    for place in range(wide // span):
        low = place * span
        keys = near_ref[:, low : low + span] + far_ref[:, low : low + span].astype(jnp.float32)
        query = query_ref[:, low : low + span]
        packed_ref[:, low : low + span] = to_half(keys * cosine - half_turn(keys) * sine)
        packed_ref[:, wide + low : wide + low + span] = to_half(
            query * cosine - half_turn(query) * sine
        )
    grad = product(packed_ref[...], weight_ref[...], pair_form)
    coded = coded_ref[...].astype(jnp.float32)
    normed, scale = centered(started(coded, vec_ref[0:1, :]))
    swell = grad * (1.0 + vec_ref[2:3, :]) * vec_ref[1:2, :]
    level = jnp.mean(swell, -1, keepdims=True)
    slope = jnp.mean(swell * normed, -1, keepdims=True)
    start_grad = scale * (swell - level - normed * slope)
    start_grad_ref[...] = to_half(start_grad)

    @pl.when(step == 0)
    def _():
        sums_ref[...] = jnp.zeros_like(sums_ref)

    sums_ref[0:1, :] += jnp.sum(grad, 0, keepdims=True)
    sums_ref[1:2, :] += jnp.sum(grad * normed, 0, keepdims=True)
    sums_ref[2:3, :] += jnp.sum(jnp.where(coded > 1e29, start_grad, 0.0), 0, keepdims=True)


def exit_stage(query_grad, near_grad, far_grad, cosine, sine, coded, vectors, weight, block):
    count, width = coded.shape
    span = cosine.shape[1]
    wide = near_grad.shape[1]
    row = pl.BlockSpec((block, width), lambda step: (step, 0))
    table = pl.BlockSpec((block, span), lambda step: (step, 0))
    piece = pl.BlockSpec((block, wide), lambda step: (step, 0))
    both = pl.BlockSpec((block, 2 * wide), lambda step: (step, 0))
    return pl.pallas_call(
        exit_kernel,
        grid=(count // block,),
        in_specs=[piece, piece, piece, table, table, row, whole(vectors.shape), whole(weight.shape)],
        out_specs=[row, both, whole((8, width))],
        out_shape=[
            jax.ShapeDtypeStruct((count, width), jnp.bfloat16),
            jax.ShapeDtypeStruct((count, 2 * wide), jnp.bfloat16),
            jax.ShapeDtypeStruct((8, width), jnp.float32),
        ],
        compiler_params=params(),
        cost_estimate=pl.CostEstimate(
            flops=4 * count * width * wide, bytes_accessed=12 * count * width, transcendentals=0
        ),
        name="exit",
    )(query_grad, near_grad, far_grad, cosine, sine, coded, vectors, weight)


def plane_shards(
    tokens,
    cotangent,
    time_index,
    absorbed,
    time_table,
    ada_weight,
    ada_bias,
    attn_gain,
    qkv_weight,
    out_weight,
    mlp_gain,
    up_weight,
    up_bias,
    down_weight,
    down_bias,
    mask_vector,
):
    batch, rows, width = tokens.shape
    layers = lax.axis_size("fsdp")
    places = lax.axis_size("ctx")
    chips = places // 2
    devices = layers * places
    head = width // H
    span = 2 * head
    heads = H // chips
    part = width // chips
    hidden = up_weight.shape[1]
    slab = hidden // layers
    slim = slab // chips
    count = rows * layers
    total = count * chips
    level = lax.axis_index("fsdp")
    place = lax.axis_index("ctx")
    chip = place // 2
    core = place % 2
    wide = jnp.float32
    low_half = part // 2

    def across(value):
        return [picked(value, level)] + [
            mirrored(picked(value, level ^ flip), "fsdp", flip) for flip in range(1, layers)
        ]

    def around(value):
        return [value] + [mirrored(value, "ctx", 2 * flip) for flip in range(1, chips)]

    local = time_index[:, None] - level * time_table.shape[0]
    onehot = (local == jnp.arange(time_table.shape[0], dtype=jnp.int32)[None, :]).astype(wide)
    raw_part = to_half(product(to_half(onehot), time_table))
    share = ada_bias.shape[0] * layers // devices
    ada_cut = lax.dynamic_slice_in_dim(ada_weight, place * layers * share, layers * share, 1)
    ada_cut = jnp.swapaxes(ada_cut.reshape(-1, layers, share), 0, 1).reshape(layers, -1)
    shared = jnp.concatenate(
        [
            raw_part.reshape(-1),
            mask_vector,
            attn_gain,
            mlp_gain,
            down_bias,
            lax.dynamic_slice_in_dim(up_bias, chip * slim, slim),
        ]
    )
    packet = jnp.concatenate(
        [jnp.broadcast_to(shared, (layers, shared.shape[0])), ada_cut], 1
    )
    packet = lax.all_to_all(packet, "fsdp", 0, 0, tiled=True)
    edges = [raw_part.size] + [mask_vector.shape[0]] * 4 + [slim, ada_cut.shape[1]]
    fields, at = [], 0
    for size in edges:
        fields.append(packet[:, at : at + size].astype(wide))
        at += size
    raw_time = jnp.sum(fields[0], 0).reshape(batch, -1)
    mask_full, attn_gain_full, mlp_gain_full, down_bias_full, up_bias_own = [
        field.reshape(-1) for field in fields[1:6]
    ]
    ada_cut = fields[6].reshape(-1, share)
    cond, silu_pull = jax.vjp(jax.nn.silu, raw_time)
    slice_rows = ada_weight.shape[0]
    cond_own = lax.dynamic_slice_in_dim(cond, level * slice_rows, slice_rows, 1)
    mod_part = jnp.dot(cond_own, ada_weight.astype(wide), precision=precise)
    bias_row = lax.dynamic_update_slice(
        jnp.zeros((mod_part.shape[1],), wide), ada_bias.astype(wide), (level * ada_bias.shape[0],)
    )
    mod_part = mod_part + bias_row[None, :]
    modulation = jnp.sum(lax.all_to_all(mod_part, "fsdp", 0, 0, tiled=True), 0).reshape(6, width)
    shift_attn, scale_attn, gate_attn, shift_mlp, scale_mlp, gate_mlp = modulation
    vectors = jnp.stack(
        [
            mask_full,
            attn_gain_full,
            scale_attn,
            shift_attn,
            gate_attn,
            mlp_gain_full,
            scale_mlp,
            shift_mlp,
            gate_mlp,
        ]
        + [jnp.zeros_like(mask_full)] * 7
    )

    coded = jnp.where((absorbed == 1)[..., None], to_half(jnp.float32(outlier)), tokens)
    coded = jnp.concatenate(around(jnp.concatenate(across(coded), 0)), 0)

    def half_rows(value):
        return lax.dynamic_slice_in_dim(value, core * low_half, low_half, 0)

    def collected(value):
        mine = jnp.stack(
            [value] + [mirrored(value, "fsdp", flip) for flip in range(1, layers)]
        )
        return mine, mirrored(mine, "ctx", 1)

    def ordered(mine, other, flip):
        blocks = []
        for far in range(layers):
            first, second = picked(mine, far ^ flip), picked(other, far ^ flip)
            blocks += [jnp.where(core == 0, first, second), jnp.where(core == 0, second, first)]
        return jnp.concatenate(blocks, 0)

    qkv_own = picked(qkv_weight.reshape(-1, 3, chips, part), chip, 2)
    qkv_full = ordered(*collected(half_rows(qkv_own.reshape(-1, 3 * part))), level)
    qkv_full = qkv_full.reshape(width, 3, heads, head)
    attn_weight = jnp.concatenate(
        [
            jnp.stack([qkv_full[:, 1], qkv_full[:, 2]], 2).reshape(width, heads * span),
            jnp.stack([qkv_full[:, 0], jnp.zeros_like(qkv_full[:, 0])], 2).reshape(
                width, heads * span
            ),
        ],
        1,
    )
    stops = [place ^ (2 * flip) for flip in range(chips)]
    steps = [level ^ flip for flip in range(layers)]
    offsets = jnp.stack([(stop * layers + step) * rows for stop in stops for step in steps])
    positions = (offsets[:, None] + jnp.arange(rows, dtype=jnp.int32)[None, :]).reshape(-1)
    freqs = 10000.0 ** (-2.0 * jnp.arange(head // 2, dtype=wide) / head)
    angles = positions.astype(wide)[:, None] * freqs[None, :]
    cosine, sine = jnp.cos(angles), jnp.sin(angles)
    ones, zeros = jnp.ones((total, head), wide), jnp.zeros((total, head), wide)
    cosine = jnp.concatenate([cosine, cosine, ones], 1)
    sine = jnp.concatenate([-sine, sine, zeros], 1)

    mixed_attn, near, query = entry(coded, vectors, attn_weight, cosine, sine, count)
    far = mirrored(near, "ctx", 1)
    cot = jnp.concatenate(around(jnp.concatenate(across(cotangent), 0)), 0)
    up_cut = picked(up_weight.reshape(-1, layers, chips, slim), chip, 2).reshape(-1, slab)
    down_cut = lax.dynamic_slice_in_dim(down_weight, chip * slim, slim, 0)
    dense = jnp.concatenate([half_rows(out_weight), half_rows(up_cut), half_rows(down_cut)], 1)
    mine, other = collected(dense)
    out_full = ordered(mine[..., :width], other[..., :width], level ^ chip)
    up_full = ordered(mine[..., width : width + slab], other[..., width : width + slab], level)
    down_full = ordered(mine[..., width + slab :], other[..., width + slab :], level)

    chunk = min(512, total)
    out, weights, inverse = attend(query, near, far, span, count, chunk)
    outs = around(out)
    back, hidden_own, mixed_mlp, upper_grad, lowered_grad, attn, bias_sum = middle_stage(
        outs, coded, cot, vectors, up_bias_own[None, :], out_full, up_full, down_full, count
    )

    def blocks_of(value):
        return [value[flip * count : (flip + 1) * count] for flip in range(chips)]

    def scattered(value):
        pieces = blocks_of(value)
        return [pieces[0]] + [mirrored(pieces[flip], "ctx", 2 * flip) for flip in range(1, chips)]

    backs = scattered(back)
    coded_own, cot_own = coded[:count], cot[:count]
    middle_grad, attn_grad, side, mlp_sums = turn_stage(
        backs, coded_own, cot_own, attn, vectors, out_full
    )
    grad_down = product(hidden_own, lowered_grad, slim_form)
    grad_up = product(mixed_mlp, upper_grad, slim_form)
    lowered_parts = scattered(to_half(product(hidden_own, down_full)))
    lowered = sum(piece.astype(wide) for piece in lowered_parts) + down_bias_full
    grad_out = cot_own.astype(wide)
    start = started(coded_own.astype(wide), mask_full)
    output = start + gate_attn * attn + gate_mlp * lowered
    gate_mlp_sum = jnp.sum(grad_out * lowered, 0)
    down_bias_sum = jnp.sum(lowered_grad[:count].astype(wide), 0)

    sides = [side[flip * part : (flip + 1) * part] for flip in range(chips)]
    grad_side = jnp.concatenate(
        [sides[0]] + [mirrored(sides[flip], "ctx", 2 * flip) for flip in range(1, chips)], 1
    )
    own_side = jnp.concatenate(
        [outs[flip][:, flip * count : (flip + 1) * count] for flip in range(chips)], 0
    )
    grad_out_weight = product(own_side, attn_grad)
    query_grad, near_grad, far_grad = attend_back(
        query, grad_side, out, weights, inverse, near, far, span, count, chunk
    )
    far_grad = mirrored(far_grad, "ctx", 1)
    start_part, packed, attn_sums = exit_stage(
        query_grad, near_grad, far_grad, cosine, sine, coded, vectors, attn_weight, count
    )
    start_grad = middle_grad + sum(piece.astype(wide) for piece in scattered(start_part))

    def home(value):
        pieces = [to_half(value[flip * rows : (flip + 1) * rows]) for flip in range(layers)]
        landed = jnp.stack(
            [pieces[0]]
            + [mirrored(pieces[flip], "fsdp", flip) for flip in range(1, layers)]
        )
        return jnp.stack([picked(landed, level ^ part_of) for part_of in range(layers)])

    output = home(output).astype(wide)
    grad_tokens = jnp.where((absorbed == 1)[..., None], 0.0, home(start_grad).astype(wide))

    grad_qkv = product(mixed_attn, packed, slim_form).reshape(width, 2, heads, 2, head)
    grad_qkv = jnp.stack([grad_qkv[:, 1, :, 0], grad_qkv[:, 0, :, 0], grad_qkv[:, 0, :, 1]], 1)
    grad_qkv = grad_qkv.reshape(width, 3 * part)

    def gathered(value, axis):
        kept = picked(value, core, axis)
        sent = to_half(picked(value, 1 - core, axis))
        return kept + mirrored(sent, "ctx", 1).astype(wide)

    def over_layers(value, axis):
        kept = picked(value, level, axis)
        for flip in range(1, layers):
            sent = to_half(picked(value, level ^ flip, axis))
            kept = kept + mirrored(sent, "fsdp", flip).astype(wide)
        return kept

    def row_blocks(value):
        split = value.reshape(chips, 2, layers, -1, value.shape[1])
        return over_layers(gathered(split, 1), 1)

    def columns(value):
        blocks = to_half(row_blocks(value))
        landed = jnp.stack(
            [picked(blocks, chip)]
            + [mirrored(picked(blocks, chip ^ flip), "ctx", 2 * flip) for flip in range(1, chips)]
        )
        return jnp.stack([picked(landed, chip ^ source) for source in range(chips)]).astype(wide)

    grad_qkv = columns(grad_qkv)
    fine = grad_qkv.shape[1]
    grad_qkv = jnp.moveaxis(grad_qkv.reshape(chips, fine, 3, part), 0, 2).reshape(fine, -1)
    grad_up = columns(grad_up)
    grad_up = jnp.moveaxis(grad_up.reshape(chips, fine, layers, slim), 0, 2).reshape(fine, -1)
    pieces = row_blocks(grad_out_weight)
    grad_out_weight = pieces[0] + sum(
        mirrored(to_half(pieces[flip]), "ctx", 2 * flip).astype(wide) for flip in range(1, chips)
    )
    grad_down = grad_down.reshape(layers, 2, -1, width)
    grad_down = over_layers(gathered(grad_down, 1), 0)
    routes = []
    for source in range(chips):
        for side_of in range(2):
            for floor in range(layers):
                block_of = (floor * chips + source) * 2 + side_of
                routes.append(((source * 2 + side_of) * layers + floor, block_of))
    grad_down = lax.ppermute(to_half(grad_down), ("ctx", "fsdp"), routes).astype(wide)

    scale_sum = attn_gain_full * attn_sums[1]
    mlp_scale_sum = mlp_gain_full * mlp_sums[1]
    grad_mod = jnp.concatenate(
        [attn_sums[0], scale_sum, mlp_sums[2], mlp_sums[0], mlp_scale_sum, gate_mlp_sum]
    )
    up_bias_sum = jnp.where(
        (jnp.arange(chips) == chip)[None, :, None], bias_sum[0].reshape(layers, 1, slim), 0.0
    )
    tiny = [
        grad_mod,
        (1.0 + scale_attn) * attn_sums[1],
        (1.0 + scale_mlp) * mlp_sums[1],
        down_bias_sum,
        attn_sums[2] + mlp_sums[3],
        up_bias_sum.reshape(-1),
    ]
    parcel = jnp.concatenate([value.reshape(devices, -1) for value in tiny], 1)
    parcel = lax.all_to_all(parcel, ("ctx", "fsdp"), 0, 0, tiled=True)
    mod_own = jnp.sum(parcel[:, :share].reshape(places, layers, share), 0)
    grad_ada_bias = jnp.sum(mod_own, 0)
    sums = jnp.sum(parcel[:, share:], 0)
    ends = [value.size // devices for value in tiny[1:]]
    small, at = [], 0
    for size in ends:
        small.append(sums[at : at + size])
        at += size
    grad_attn_gain, grad_mlp_gain, grad_down_bias, grad_mask, grad_up_bias = small
    cond_part = lax.dot_general(
        mod_own, ada_cut, pair_form, precision=precise, preferred_element_type=wide
    )
    notice = jnp.concatenate([mod_own.reshape(-1), cond_part.reshape(-1)])
    notice = jnp.broadcast_to(notice, (devices, notice.shape[0]))
    notice = lax.all_to_all(notice, ("ctx", "fsdp"), 0, 0, tiled=True)
    mod_full = jnp.swapaxes(
        notice[:, : batch * share].reshape(devices, batch, share), 0, 1
    ).reshape(batch, -1)
    grad_cond = jnp.sum(notice[:, batch * share :], 0).reshape(batch, -1)
    grad_raw = silu_pull(grad_cond)[0]
    device = place * layers + level
    cond_rows = cond.shape[1] // devices
    cond_cut = lax.dynamic_slice_in_dim(cond, device * cond_rows, cond_rows, 1)
    grad_ada_weight = jnp.dot(cond_cut.T, mod_full, precision=precise)
    table_rows = time_table.shape[0] * layers // devices
    picks = time_index[None, :] == (
        device * table_rows + jnp.arange(table_rows, dtype=jnp.int32)
    )[:, None]
    grad_table = jnp.dot(picks.astype(wide), grad_raw, precision=precise)
    return (
        output,
        grad_tokens,
        grad_table,
        grad_ada_weight,
        grad_ada_bias,
        grad_attn_gain,
        grad_qkv,
        grad_out_weight,
        grad_mlp_gain,
        grad_up,
        grad_up_bias,
        grad_down,
        grad_down_bias,
        grad_mask,
    )


def suits(tokens, up_weight):
    batch, rows, width = tokens.shape
    layers, places = lax.axis_size("fsdp"), lax.axis_size("ctx")
    chips = places // 2
    return (
        places == 8
        and layers == 4
        and batch == layers
        and H % chips == 0
        and width == 64 * H
        and rows * layers == 256
        and up_weight.shape[1] == layers * width
    )


def shards(*arrays):
    if suits(arrays[0], arrays[11]):
        return plane_shards(*arrays)
    return ring_shards(*arrays)


def solution(mesh):
    return jax.shard_map(
        shards,
        mesh=mesh,
        in_specs=(
            P(None, ("ctx", "fsdp"), None),
            P(None, ("ctx", "fsdp"), None),
            P(),
            P(None, ("ctx", "fsdp")),
            P("fsdp", None),
            P("fsdp", None),
            P("fsdp"),
            P("fsdp"),
            P("fsdp", None),
            P("fsdp", None),
            P("fsdp"),
            P("fsdp", None),
            P("fsdp"),
            P("fsdp", None),
            P("fsdp"),
            P("fsdp"),
        ),
        out_specs=(
            P(None, ("ctx", "fsdp"), None),
            P(None, ("ctx", "fsdp"), None),
            P(("ctx", "fsdp"), None),
            P(("ctx", "fsdp"), None),
            P(("ctx", "fsdp")),
            P(("ctx", "fsdp")),
            P(("ctx", "fsdp"), None),
            P(("ctx", "fsdp"), None),
            P(("ctx", "fsdp")),
            P(("ctx", "fsdp"), None),
            P(("ctx", "fsdp")),
            P(("ctx", "fsdp"), None),
            P(("ctx", "fsdp")),
            P(("ctx", "fsdp")),
        ),
        check_vma=False,
    )
```

```python
import functools
import math

import jax
import jax.numpy as jnp
from jax import lax
from jax.experimental import pallas as pl
from jax.experimental.pallas import tpu as pltpu
from jax.sharding import Mesh
from jax.sharding import PartitionSpec as P

H = 12


epsilon = 1e-05
precise = lax.Precision.HIGHEST
lowest = -1e30


def shifted(value, axis, steps):
    count = lax.axis_size(axis)
    pairs = [(source, (source + steps) % count) for source in range(count)]
    return lax.ppermute(value, axis, pairs)


def combined_all(value, axis, join):
    pieces = jax.tree.map(lambda part: lax.all_gather(part, axis), value)
    head = jax.tree.map(lambda part: part[0], pieces)
    tail = jax.tree.map(lambda part: part[1:], pieces)
    subtotal, _ = lax.scan(lambda subtotal, slab: (join(subtotal, slab), None), head, tail)
    return subtotal


def to_half(values):
    return values.astype(jnp.bfloat16)


def normalize(values):
    center = values - jnp.mean(values, -1, keepdims=True)
    spread = jnp.mean(center * center, -1, keepdims=True)
    return center * lax.rsqrt(spread + epsilon)


def premix(values, gain, shift, scale):
    return normalize(values) * gain * (1.0 + scale) + shift


def rotary(positions, head):
    half = head // 2
    freqs = 10000.0 ** (-2.0 * jnp.arange(half, dtype=jnp.float32) / head)
    angles = positions[:, None] * freqs[None, :]
    cosine = jnp.concatenate([jnp.cos(angles), jnp.cos(angles)], -1)
    sine = jnp.concatenate([jnp.sin(angles), jnp.sin(angles)], -1)
    return (cosine, sine)


def turn_half(values):
    half = values.shape[-1] // 2
    return jnp.concatenate([-values[..., half:], values[..., :half]], -1)


def rotate(values, cosine, sine, direction):
    return (
        values * cosine[None, :, None, :] + direction * turn_half(values) * sine[None, :, None, :]
    )


def fetch_attn(time_table, ada_weight, ada_bias, attn_gain, qkv_weight, out_weight, mask_vector):
    return (
        lax.all_gather(time_table, "fsdp", axis=0, tiled=True),
        lax.all_gather(ada_weight, "fsdp", axis=0, tiled=True),
        lax.all_gather(ada_bias, "fsdp", axis=0, tiled=True),
        lax.all_gather(attn_gain, "fsdp", axis=0, tiled=True),
        lax.all_gather(qkv_weight, "fsdp", axis=0, tiled=True),
        lax.all_gather(out_weight, "fsdp", axis=0, tiled=True),
        lax.all_gather(mask_vector, "fsdp", axis=0, tiled=True),
    )


def fetch_mlp(mlp_gain, up_weight, up_bias, down_weight, down_bias):
    return (
        lax.all_gather(mlp_gain, "fsdp", axis=0, tiled=True),
        lax.all_gather(up_weight, "fsdp", axis=0, tiled=True),
        lax.all_gather(up_bias, "fsdp", axis=0, tiled=True),
        lax.all_gather(down_weight, "fsdp", axis=0, tiled=True),
        lax.all_gather(down_bias, "fsdp", axis=0, tiled=True),
    )


def online(carry, keys, values, query4):
    best, total, summed = carry
    batch, count, heads, head = query4.shape
    key4 = keys.reshape(batch, -1, heads, head)
    value4 = values.reshape(batch, -1, heads, head)
    scores = jnp.einsum(
        "bqhd,bkhd->bqhk", query4, key4, preferred_element_type=jnp.float32
    ) * head ** (-0.5)
    raised = jnp.maximum(best, jnp.max(scores, -1))
    factor = jnp.exp(best - raised)
    weights = jnp.exp(scores - raised[..., None])
    total = total * factor + jnp.sum(weights, -1)
    update = jnp.einsum("bqhk,bkhd->bqhd", weights, value4, preferred_element_type=jnp.float32)
    summed = summed.reshape(batch, count, heads, head) * factor[..., None] + update
    return (raised, total, summed.reshape(batch, count, heads * head))


def fold_keys(carry, piece, query4):
    keys, values = piece
    count = keys.shape[1]
    splits = 1
    while count // splits > 256 and count % (splits * 2) == 0:
        splits = splits * 2
    batch = keys.shape[0]
    width = keys.shape[2]
    key_blocks = jnp.moveaxis(keys.reshape(batch, splits, count // splits, width), 1, 0)
    value_blocks = jnp.moveaxis(values.reshape(batch, splits, count // splits, width), 1, 0)

    def advance(state, pair):
        return (online(state, pair[0], pair[1], query4), None)

    carry, unused = lax.scan(advance, carry, (key_blocks, value_blocks))
    return carry


def combine(first, second):
    raised = jnp.maximum(first[0], second[0])
    left = jnp.exp(first[0] - raised)
    right = jnp.exp(second[0] - raised)
    batch, count, heads = raised.shape
    total = first[1] * left + second[1] * right
    summed = (
        first[2].reshape(batch, count, heads, -1) * left[..., None]
        + second[2].reshape(batch, count, heads, -1) * right[..., None]
    )
    return (raised, total, summed.reshape(batch, count, -1))


def block_grads(keys, values, query4, grad4, logsum, delta):
    batch, count, heads, head = query4.shape
    key4 = keys.reshape(batch, -1, heads, head)
    value4 = values.reshape(batch, -1, heads, head)
    factor = head ** (-0.5)
    scores = (
        jnp.einsum("bqhd,bkhd->bqhk", query4, key4, preferred_element_type=jnp.float32) * factor
    )
    probs = jnp.exp(scores - logsum[..., None])
    grad_probs = jnp.einsum("bqhd,bkhd->bqhk", grad4, value4, preferred_element_type=jnp.float32)
    grad_scores = to_half(probs * (grad_probs - delta[..., None]))
    query_add = (
        jnp.einsum("bqhk,bkhd->bqhd", grad_scores, key4, preferred_element_type=jnp.float32)
        * factor
    )
    key_add = (
        jnp.einsum("bqhk,bqhd->bkhd", grad_scores, query4, preferred_element_type=jnp.float32)
        * factor
    )
    value_add = jnp.einsum("bqhk,bqhd->bkhd", probs, grad4, preferred_element_type=jnp.float32)
    return (
        query_add.reshape(batch, count, -1),
        key_add.reshape(keys.shape),
        value_add.reshape(values.shape),
    )


def pass_keys(keys, values):
    return shifted((keys, values), "ctx", 1)


def pass_grads(key_grad, value_grad):
    return (
        shifted(key_grad.astype(jnp.bfloat16), "ctx", 1).astype(key_grad.dtype),
        shifted(value_grad.astype(jnp.bfloat16), "ctx", 1).astype(value_grad.dtype),
    )


def ring_shards(
    tokens,
    cotangent,
    time_index,
    absorbed,
    time_table,
    ada_weight,
    ada_bias,
    attn_gain,
    qkv_weight,
    out_weight,
    mlp_gain,
    up_weight,
    up_bias,
    down_weight,
    down_bias,
    mask_vector,
):
    batch, rows, width = tokens.shape
    heads = H
    head = width // heads
    fsdp_count = lax.axis_size("fsdp")
    cycle_count = lax.axis_size("ctx")
    stop_place = lax.axis_index("fsdp")
    device_place = lax.axis_index("ctx") * fsdp_count + stop_place
    table_full, ada_full, ada_bias_full, attn_gain_full, qkv_full, out_full, mask_full = fetch_attn(
        time_table, ada_weight, ada_bias, attn_gain, qkv_weight, out_weight, mask_vector
    )
    steps_total = table_full.shape[0]
    onehot = (time_index[:, None] == jnp.arange(steps_total, dtype=jnp.int32)[None, :]).astype(
        jnp.float32
    )
    raw_time = jnp.dot(onehot, table_full.astype(jnp.float32), precision=precise)
    cond, silu_pull = jax.vjp(jax.nn.silu, raw_time)
    modulation = jnp.dot(
        cond, ada_full.astype(jnp.float32), precision=precise
    ) + ada_bias_full.astype(jnp.float32)
    pieces = [modulation[:, None, part * width : (part + 1) * width] for part in range(6)]
    shift_attn, scale_attn, gate_attn, shift_mlp, scale_mlp, gate_mlp = pieces
    masked = (absorbed == 1)[..., None]
    start = jnp.where(masked, mask_full.astype(jnp.float32), tokens.astype(jnp.float32))
    attn_gain_wide = attn_gain_full.astype(jnp.float32)
    mixed_attn = to_half(premix(start, attn_gain_wide, shift_attn, scale_attn))
    qkv = jnp.einsum("btd,de->bte", mixed_attn, qkv_full, preferred_element_type=jnp.float32)
    positions = (device_place * rows + jnp.arange(rows, dtype=jnp.int32)).astype(jnp.float32)
    cosine, sine = rotary(positions, head)
    query_own = to_half(
        rotate(qkv[..., :width].reshape(batch, rows, heads, head), cosine, sine, 1.0)
    ).reshape(batch, rows, width)
    key_own = to_half(
        rotate(qkv[..., width : 2 * width].reshape(batch, rows, heads, head), cosine, sine, 1.0)
    ).reshape(batch, rows, width)
    value_own = to_half(qkv[..., 2 * width :])
    query_stop = lax.all_gather(query_own, "fsdp", axis=1, tiled=True)
    stop_rows = query_stop.shape[1]
    query4 = query_stop.reshape(batch, stop_rows, heads, head)
    start_state = (
        jnp.full((batch, stop_rows, heads), lowest, jnp.float32),
        jnp.zeros((batch, stop_rows, heads), jnp.float32),
        jnp.zeros((batch, stop_rows, width), jnp.float32),
    )
    best, total, summed = fold_keys(
        start_state,
        (
            lax.all_gather(key_own, "ctx", axis=1, tiled=True),
            lax.all_gather(value_own, "ctx", axis=1, tiled=True),
        ),
        query4,
    )
    best, total, summed = combined_all((best, total, summed), "fsdp", combine)
    logsum = best + jnp.log(total)
    attended_stop = (summed.reshape(batch, stop_rows, heads, head) / total[..., None]).reshape(
        batch, stop_rows, width
    )
    attended = lax.dynamic_slice_in_dim(attended_stop, stop_place * rows, rows, 1)
    attended_low = to_half(attended)
    attn = jnp.einsum("btd,de->bte", attended_low, out_full, preferred_element_type=jnp.float32)
    middle = start + gate_attn * attn
    mlp_gain_full, up_full, up_bias_full, down_full, down_bias_full = fetch_mlp(
        mlp_gain, up_weight, up_bias, down_weight, down_bias
    )
    mlp_gain_wide = mlp_gain_full.astype(jnp.float32)
    mixed_mlp = to_half(premix(middle, mlp_gain_wide, shift_mlp, scale_mlp))
    upper = jnp.einsum(
        "btd,df->btf", mixed_mlp, up_full, preferred_element_type=jnp.float32
    ) + up_bias_full.astype(jnp.float32)
    hidden = to_half(jax.nn.gelu(upper, approximate=True))
    lowered = jnp.einsum(
        "btf,fd->btd", hidden, down_full, preferred_element_type=jnp.float32
    ) + down_bias_full.astype(jnp.float32)
    output = middle + gate_mlp * lowered
    mlp_gain_full, up_full, up_bias_full, down_full, down_bias_full = fetch_mlp(
        mlp_gain, up_weight, up_bias, down_weight, down_bias
    )
    grad_out = cotangent.astype(jnp.float32)
    grad_lowered = to_half(grad_out * gate_mlp)
    grad_gate_mlp = jnp.sum(grad_out * lowered, 1)
    grad_down_bias = jnp.sum(grad_lowered.astype(jnp.float32), (0, 1))
    grad_down_weight = jnp.einsum(
        "btf,btd->fd", hidden, grad_lowered, preferred_element_type=jnp.float32
    )
    grad_hidden = jnp.einsum(
        "btd,fd->btf", grad_lowered, down_full, preferred_element_type=jnp.float32
    )
    gelu_pull = jax.vjp(lambda values: jax.nn.gelu(values, approximate=True), upper)[1]
    grad_upper = to_half(gelu_pull(grad_hidden)[0])
    grad_up_bias = jnp.sum(grad_upper.astype(jnp.float32), (0, 1))
    grad_up_weight = jnp.einsum(
        "btd,btf->df", mixed_mlp, grad_upper, preferred_element_type=jnp.float32
    )
    grad_mixed_mlp = jnp.einsum(
        "btf,df->btd", grad_upper, up_full, preferred_element_type=jnp.float32
    )
    mlp_pull = jax.vjp(premix, middle, mlp_gain_wide, shift_mlp, scale_mlp)[1]
    grad_middle_part, grad_mlp_gain, grad_shift_mlp, grad_scale_mlp = mlp_pull(grad_mixed_mlp)
    grad_middle = grad_out + grad_middle_part
    table_full, ada_full, ada_bias_full, attn_gain_full, qkv_full, out_full, mask_full = fetch_attn(
        time_table, ada_weight, ada_bias, attn_gain, qkv_weight, out_weight, mask_vector
    )
    grad_attn = to_half(grad_middle * gate_attn)
    grad_gate_attn = jnp.sum(grad_middle * attn, 1)
    grad_out_weight = jnp.einsum(
        "btd,bte->de", attended_low, grad_attn, preferred_element_type=jnp.float32
    )
    grad_attended = to_half(
        jnp.einsum("bte,de->btd", grad_attn, out_full, preferred_element_type=jnp.float32)
    )
    grad_stop = lax.all_gather(grad_attended, "fsdp", axis=1, tiled=True)
    grad4 = grad_stop.reshape(batch, stop_rows, heads, head)
    delta = jnp.sum(
        grad4.astype(jnp.float32) * attended_stop.reshape(batch, stop_rows, heads, head), -1
    )
    zeros_stop = jnp.zeros((batch, stop_rows, width), jnp.float32)

    def cycle_turn(position, state):
        keys, values, key_grad, value_grad, query_grad = state
        query_add, key_add, value_add = block_grads(keys, values, query4, grad4, logsum, delta)
        keys, values = pass_keys(keys, values)
        key_grad, value_grad = pass_grads(key_grad + key_add, value_grad + value_add)
        return (keys, values, key_grad, value_grad, query_grad + query_add)

    zeros_own = jnp.zeros((batch, rows, width), jnp.float32)
    keys, values, key_grad, value_grad, query_sum = lax.fori_loop(
        0, cycle_count - 1, cycle_turn, (key_own, value_own, zeros_own, zeros_own, zeros_stop)
    )
    query_add, key_add, value_add = block_grads(keys, values, query4, grad4, logsum, delta)
    key_grad, value_grad = pass_grads(key_grad + key_add, value_grad + value_add)
    query_partial = query_sum + query_add
    query_grad = lax.psum_scatter(
        query_partial.astype(jnp.bfloat16), "fsdp", scatter_dimension=1, tiled=True
    ).astype(jnp.float32)
    grad_query = rotate(query_grad.reshape(batch, rows, heads, head), cosine, sine, -1.0).reshape(
        batch, rows, width
    )
    grad_key = rotate(key_grad.reshape(batch, rows, heads, head), cosine, sine, -1.0).reshape(
        batch, rows, width
    )
    grad_qkv = to_half(jnp.concatenate([grad_query, grad_key, value_grad], -1))
    grad_qkv_weight = jnp.einsum(
        "btd,bte->de", mixed_attn, grad_qkv, preferred_element_type=jnp.float32
    )
    grad_mixed_attn = jnp.einsum(
        "bte,de->btd", grad_qkv, qkv_full, preferred_element_type=jnp.float32
    )
    attn_pull = jax.vjp(premix, start, attn_gain_wide, shift_attn, scale_attn)[1]
    grad_start_part, grad_attn_gain, grad_shift_attn, grad_scale_attn = attn_pull(grad_mixed_attn)
    grad_start = grad_middle + grad_start_part
    grad_tokens = jnp.where(masked, 0.0, grad_start)
    grad_mask_vector = jnp.sum(jnp.where(masked, grad_start, 0.0), (0, 1))
    grad_modulation = jnp.concatenate(
        [
            grad_shift_attn[:, 0],
            grad_scale_attn[:, 0],
            grad_gate_attn,
            grad_shift_mlp[:, 0],
            grad_scale_mlp[:, 0],
            grad_gate_mlp,
        ],
        -1,
    )
    grad_ada_bias = jnp.sum(grad_modulation, 0)
    grad_ada_weight = jnp.dot(cond.T, grad_modulation, precision=precise)
    grad_cond = jnp.dot(grad_modulation, ada_full.astype(jnp.float32).T, precision=precise)
    grad_raw = silu_pull(grad_cond)[0]
    grad_table = jnp.dot(onehot.T, grad_raw, precision=precise)
    summed_grads = (
        lax.psum_scatter(grad_table, ("ctx", "fsdp"), scatter_dimension=0, tiled=True),
        lax.psum_scatter(grad_ada_weight, ("ctx", "fsdp"), scatter_dimension=0, tiled=True),
        lax.psum_scatter(grad_ada_bias, ("ctx", "fsdp"), scatter_dimension=0, tiled=True),
        lax.psum_scatter(grad_attn_gain, ("ctx", "fsdp"), scatter_dimension=0, tiled=True),
        lax.psum_scatter(grad_qkv_weight, ("ctx", "fsdp"), scatter_dimension=0, tiled=True),
        lax.psum_scatter(grad_out_weight, ("ctx", "fsdp"), scatter_dimension=0, tiled=True),
        lax.psum_scatter(grad_mlp_gain, ("ctx", "fsdp"), scatter_dimension=0, tiled=True),
        lax.psum_scatter(grad_up_weight, ("ctx", "fsdp"), scatter_dimension=0, tiled=True),
        lax.psum_scatter(grad_up_bias, ("ctx", "fsdp"), scatter_dimension=0, tiled=True),
        lax.psum_scatter(grad_down_weight, ("ctx", "fsdp"), scatter_dimension=0, tiled=True),
        lax.psum_scatter(grad_down_bias, ("ctx", "fsdp"), scatter_dimension=0, tiled=True),
        lax.psum_scatter(grad_mask_vector, ("ctx", "fsdp"), scatter_dimension=0, tiled=True),
    )
    (
        grad_table,
        grad_ada_weight,
        grad_ada_bias,
        grad_attn_gain,
        grad_qkv_weight,
        grad_out_weight,
        grad_mlp_gain,
        grad_up_weight,
        grad_up_bias,
        grad_down_weight,
        grad_down_bias,
        grad_mask_vector,
    ) = summed_grads
    return (
        output,
        grad_tokens,
        grad_table,
        grad_ada_weight,
        grad_ada_bias,
        grad_attn_gain,
        grad_qkv_weight,
        grad_out_weight,
        grad_mlp_gain,
        grad_up_weight,
        grad_up_bias,
        grad_down_weight,
        grad_down_bias,
        grad_mask_vector,
    )

outlier = 1e30
pair_form = (((1,), (1,)), ((), ()))
plain_form = (((1,), (0,)), ((), ()))
slim_form = (((0,), (0,)), ((), ()))
curve = 0.7978845608028654
cube = 0.044715


def product(left, right, form=plain_form):
    return lax.dot_general(left, right, form, preferred_element_type=jnp.float32)


def mirrored(value, axis, flip):
    count = lax.axis_size(axis)
    return lax.ppermute(value, axis, [(place, place ^ flip) for place in range(count)])


def picked(value, place, axis=0):
    return lax.dynamic_index_in_dim(value, place, axis, keepdims=False)


def whole(shape):
    return pl.BlockSpec(shape, lambda *_: (0,) * len(shape))


def lasting(time):
    return pl.CostEstimate(flops=int(time * 1.15e9), bytes_accessed=1024, transcendentals=0)


def params(count=1, room=56):
    return pltpu.CompilerParams(
        vmem_limit_bytes=room * 1024 * 1024, dimension_semantics=("arbitrary",) * count
    )


def tied(*values):
    return lax.optimization_barrier(values)


def assembled(target, mine, other, flip, core, low, high):
    layers, size, _ = mine.shape
    for far in range(layers):
        first, second = mine[far ^ flip, :, low:high], other[far ^ flip, :, low:high]
        swap = core == 1
        target[2 * far * size : (2 * far + 1) * size, :] = jnp.where(swap, second, first)
        target[(2 * far + 1) * size : (2 * far + 2) * size, :] = jnp.where(swap, first, second)


def half_turn(values):
    lane = lax.broadcasted_iota(jnp.int32, values.shape, 1)
    span = values.shape[1]
    return jnp.where(
        lane < span // 4,
        pltpu.roll(values, span - span // 4, 1),
        pltpu.roll(values, span // 4, 1),
    )


def centered(values):
    center = values - jnp.mean(values, -1, keepdims=True)
    spread = jnp.mean(center * center, -1, keepdims=True)
    scale = lax.rsqrt(spread + epsilon)
    return center * scale, scale


def started(coded, mask_row):
    return jnp.where(coded > 1e29, mask_row, coded)


def prologue_kernel(
    flags_ref, index_ref, tokens_ref, absorbed_ref, table_ref, mask_ref, gain_ref, mlp_gain_ref,
    down_bias_ref, up_bias_ref, qkv_ref, packet_ref, pack_ref
):
    core, chip = flags_ref[1], flags_ref[2]
    batch, rows, width = tokens_ref.shape
    steps = table_ref.shape[0]
    local = lax.broadcasted_iota(jnp.int32, (8, steps), 1) + flags_ref[0] * steps
    row = lax.broadcasted_iota(jnp.int32, (8, steps), 0)
    wanted = jnp.zeros((8, steps), jnp.int32) - 1
    for order in range(batch):
        wanted = jnp.where(row == order, index_ref[order], wanted)
    chosen = to_half(product(to_half((wanted == local).astype(jnp.float32)), table_ref[...]))
    chosen = jnp.concatenate([chosen, jnp.zeros((8, width - chosen.shape[1]), jnp.bfloat16)], 1)
    small = [
        jnp.pad(ref[...].astype(jnp.float32)[None, :], ((0, 0), (0, width - ref.shape[0])))
        for ref in (mask_ref, gain_ref, mlp_gain_ref, down_bias_ref, up_bias_ref)
    ]
    small = to_half(jnp.concatenate(small + [jnp.zeros((3, width), jnp.float32)], 0))
    diagonal = lax.broadcasted_iota(jnp.int32, (rows, rows), 0) == lax.broadcasted_iota(
        jnp.int32, (rows, rows), 1
    )
    for order in range(batch):
        line = jnp.where(diagonal, absorbed_ref[order : order + 1, :], 0)
        marked = jnp.sum(line.astype(jnp.float32), 1, keepdims=True) == 1.0
        packet_ref[order, :rows, :] = to_half(
            jnp.where(marked, outlier, tokens_ref[order].astype(jnp.float32))
        )
        packet_ref[order, rows : rows + 8, :] = chosen
        packet_ref[order, rows + 8 :, :] = small
    size = pack_ref.shape[0]
    part = width // 4
    lane = lax.broadcasted_iota(jnp.int32, (size, 128), 1)
    low_rows = pl.multiple_of(core * size, size)

    def window(base):
        begin = pl.multiple_of(base + chip * part - 64 * (chip % 2), 128)
        tile = qkv_ref[pl.ds(low_rows, size), pl.ds(begin, 256)].astype(jnp.float32)
        tile = jnp.where(chip % 2 == 1, pltpu.roll(tile, 192, 1), tile)
        return tile[:, :128], tile[:, 128:]

    def turned(tile):
        return pltpu.roll(tile, 64, 1)

    queries, keys, values = window(0), window(width), window(2 * width)
    low = lane < 64
    for order, tile in enumerate(
        [
            jnp.where(low, keys[0], turned(values[0])),
            jnp.where(low, turned(keys[0]), values[0]),
            jnp.where(low, keys[1], turned(values[1])),
            queries[0],
            jnp.where(low, queries[1], 0.0),
        ]
    ):
        pack_ref[:, order * 128 : (order + 1) * 128] = to_half(tile)


def prologue(flags, time_index, tokens, absorbed, table, small, qkv_weight):
    batch, rows, width = tokens.shape
    shape = (batch, rows + 16, width)
    smem = pl.BlockSpec(memory_space=pltpu.SMEM)
    pack = (width // 8, 5 * 128)
    return pl.pallas_call(
        prologue_kernel,
        grid=(1,),
        in_specs=[smem, smem]
        + [whole(value.shape) for value in (tokens, absorbed, table, *small, qkv_weight)],
        out_specs=[whole(shape), whole(pack)],
        out_shape=[
            jax.ShapeDtypeStruct(shape, jnp.bfloat16),
            jax.ShapeDtypeStruct(pack, jnp.bfloat16),
        ],
        compiler_params=params(room=60),
        cost_estimate=lasting(2),
        name="prologue",
    )(flags, time_index, tokens, absorbed, table, *small, qkv_weight)


def entry_kernel(
    flags_ref, coded0_ref, coded1_ref, coded2_ref, coded3_ref, vec_ref, mine_ref, other_ref,
    cos_ref, sin_ref, mixed_ref, kv_ref, query_ref, weight_ref, coded_ref
):
    @pl.when(pl.program_id(0) == 0)
    def _():
        assembled(weight_ref, mine_ref, other_ref, flags_ref[0], flags_ref[1], 0, None)

    for place, ref in enumerate((coded0_ref, coded1_ref, coded2_ref, coded3_ref)):

        @pl.when(pl.program_id(0) == place // (coded_ref.shape[0] // ref.shape[0]))
        def _(ref=ref, low=place * ref.shape[0] % coded_ref.shape[0], size=ref.shape[0]):
            coded_ref[low : low + size, :] = ref[...]

    start = started(coded_ref[...].astype(jnp.float32), vec_ref[0:1, :])
    normed, _ = centered(start)
    mixed = to_half(normed * vec_ref[1:2, :] * (1.0 + vec_ref[2:3, :]) + vec_ref[3:4, :])
    mixed_ref[...] = mixed
    both = product(mixed, weight_ref[...])
    cosine, sine = cos_ref[...], sin_ref[...]
    span = cosine.shape[1]
    wide = kv_ref.shape[1]
    heads = wide // span
    lane = lax.broadcasted_iota(jnp.int32, cosine.shape, 1)
    factor = (span // 2) ** (-0.5)
    for place in range(heads):
        values = both[:, place * span : (place + 1) * span]
        kv_ref[:, place * span : (place + 1) * span] = to_half(
            values * cosine + half_turn(values) * sine
        )
        low = wide + (place // 2) * span
        values = both[:, low : low + span]
        if place % 2:
            values = pltpu.roll(values, span // 2, 1)
        values = jnp.where(lane < span // 2, values, 0.0)
        values = to_half(values * cosine + half_turn(values) * sine)
        query_ref[:, place * span : (place + 1) * span] = values * to_half(jnp.float32(factor))


def entry(flags, coded, vectors, mine, other, cosine, sine, heads, block):
    unit, width = coded[0].shape
    count = unit * len(coded)
    span = cosine.shape[1]
    wide = heads * span
    row = pl.BlockSpec((block, width), lambda step: (step, 0))
    table = pl.BlockSpec((block, span), lambda step: (step, 0))
    piece = pl.BlockSpec((block, wide), lambda step: (step, 0))
    packed = (width, mine.shape[2])
    return pl.pallas_call(
        entry_kernel,
        grid=(count // block,),
        in_specs=[pl.BlockSpec(memory_space=pltpu.SMEM)]
        + [whole((unit, width))] * 4
        + [whole(vectors.shape), whole(mine.shape), whole(other.shape), table, table],
        out_specs=[row, piece, piece, whole(packed), row],
        out_shape=[
            jax.ShapeDtypeStruct((count, width), jnp.bfloat16),
            jax.ShapeDtypeStruct((count, wide), jnp.bfloat16),
            jax.ShapeDtypeStruct((count, wide), jnp.bfloat16),
            jax.ShapeDtypeStruct(packed, jnp.bfloat16),
            jax.ShapeDtypeStruct((count, width), jnp.bfloat16),
        ],
        compiler_params=params(room=56),
        cost_estimate=lasting(7),
        name="entry",
    )(flags, *coded, vectors, mine, other, cosine, sine)


def attend_kernel(query_ref, near_ref, far_ref, out_ref, exp_ref, inv_ref, turned, scores, *, chunk):
    count, span = near_ref.shape
    half = span // 2

    @pl.when(pl.program_id(1) == 0)
    def _():
        row = lax.broadcasted_iota(jnp.int32, (span, count), 0)
        for place, ref in enumerate((near_ref, far_ref)):
            flat = ref[...].astype(jnp.float32).T
            turned[:, place * count : (place + 1) * count] = to_half(jnp.where(row < half, 1.0, flat))

    query = query_ref[...]
    best = None
    pieces = count // chunk
    for place in range(2 * pieces):
        ref = (near_ref, far_ref)[place // pieces]
        low = (place % pieces) * chunk
        part = product(ref[low : low + chunk, :], query, pair_form)
        scores[place * chunk : (place + 1) * chunk, :] = part
        top = jnp.max(part, axis=0, keepdims=True)
        best = top if best is None else jnp.maximum(best, top)
    total = None
    for place in range(2 * pieces):
        part = to_half(jnp.exp(scores[place * chunk : (place + 1) * chunk, :] - best))
        exp_ref[0, place * chunk : (place + 1) * chunk, :] = part
        add = product(turned[:, place * chunk : (place + 1) * chunk], part)
        total = add if total is None else total + add
    inverse = 1.0 / total[0:1, :]
    out_ref[...] = to_half(total[half:, :] * inverse)
    inv_ref[0] = inverse


def attend(query, near, far, span, block, chunk):
    count = query.shape[0]
    heads = query.shape[1] // span
    keys = near.shape[0]
    stay = pl.BlockSpec((keys, span), lambda head, step: (0, head))
    return pl.pallas_call(
        functools.partial(attend_kernel, chunk=chunk),
        grid=(heads, count // block),
        in_specs=[pl.BlockSpec((block, span), lambda head, step: (step, head)), stay, stay],
        out_specs=[
            pl.BlockSpec((span // 2, block), lambda head, step: (head, step)),
            pl.BlockSpec((1, 2 * keys, block), lambda head, step: (head, 0, step)),
            pl.BlockSpec((1, 1, block), lambda head, step: (head, 0, step)),
        ],
        out_shape=[
            jax.ShapeDtypeStruct((heads * span // 2, count), jnp.bfloat16),
            jax.ShapeDtypeStruct((heads, 2 * keys, count), jnp.bfloat16),
            jax.ShapeDtypeStruct((heads, 1, count), jnp.float32),
        ],
        scratch_shapes=[
            pltpu.VMEM((span, 2 * keys), jnp.bfloat16),
            pltpu.VMEM((2 * keys, block), jnp.float32),
        ],
        compiler_params=params(2, room=56),
        cost_estimate=lasting(4),
        name="attend",
    )(query, near, far)


def attend_back_kernel(
    query_ref, side0_ref, side1_ref, side2_ref, side3_ref, out_ref, exp_ref, inv_ref, near_ref,
    far_ref, query_grad_ref, near_grad_ref, far_grad_ref, turned, sums, grad_ref, *, chunk
):
    count, span = near_ref.shape
    half = span // 2
    step = pl.program_id(1)

    @pl.when(step == 0)
    def _():
        for place, ref in enumerate((near_ref, far_ref)):
            flat = ref[...].astype(jnp.float32).T
            turned[:, place * count : (place + 1) * count] = to_half(flat)[:half]
        sums[...] = jnp.zeros_like(sums)

    size = side0_ref.shape[1]
    share = grad_ref.shape[1] // size
    for place, ref in enumerate((side0_ref, side1_ref, side2_ref, side3_ref)):

        @pl.when(step == place // share)
        def _(ref=ref, low=place % share * size):
            grad_ref[:, low : low + size] = ref[...]

    inverse = inv_ref[0]
    grad = grad_ref[...].astype(jnp.float32) * inverse
    delta = jnp.sum(grad * out_ref[...].astype(jnp.float32), axis=0, keepdims=True)
    padded = jnp.concatenate([jnp.zeros_like(grad), grad], 0)
    side = to_half(padded)
    upright = to_half(padded.T)
    query = query_ref[...]
    pieces = count // chunk
    total = None
    for place in range(2 * pieces):
        ref = (near_ref, far_ref)[place // pieces]
        low = (place % pieces) * chunk
        part = product(ref[low : low + chunk, :], side)
        weights = exp_ref[0, place * chunk : (place + 1) * chunk, :]
        grad_scores = to_half(weights.astype(jnp.float32) * (part - delta))
        sums[place * chunk : (place + 1) * chunk, :] += product(grad_scores, query) + product(
            weights, upright
        )
        add = product(turned[:, place * chunk : (place + 1) * chunk], grad_scores)
        total = add if total is None else total + add
    total = total * (half ** (-0.5))
    query_grad_ref[...] = jnp.concatenate([total, jnp.zeros_like(total)], 0).T

    @pl.when(step == pl.num_programs(1) - 1)
    def _():
        near_grad_ref[...] = sums[:count, :]
        far_grad_ref[...] = to_half(sums[count:, :])


def attend_back(query, sides, out, weights, inverse, near, far, span, block, chunk):
    count = query.shape[0]
    heads = query.shape[1] // span
    keys = near.shape[0]
    stay = pl.BlockSpec((keys, span), lambda head, step: (0, head))
    flow = pl.BlockSpec((block, span), lambda head, step: (step, head))
    flat = pl.BlockSpec((span // 2, block), lambda head, step: (head, step))
    return pl.pallas_call(
        functools.partial(attend_back_kernel, chunk=chunk),
        grid=(heads, count // block),
        in_specs=[flow]
        + [pl.BlockSpec((span // 2, count // 4), lambda head, step: (head, 0))] * 4
        + [
            flat,
            pl.BlockSpec((1, 2 * keys, block), lambda head, step: (head, 0, step)),
            pl.BlockSpec((1, 1, block), lambda head, step: (head, 0, step)),
            stay,
            stay,
        ],
        out_specs=[flow, stay, stay],
        out_shape=[
            jax.ShapeDtypeStruct((count, heads * span), jnp.float32),
            jax.ShapeDtypeStruct((keys, heads * span), jnp.float32),
            jax.ShapeDtypeStruct((keys, heads * span), jnp.bfloat16),
        ],
        scratch_shapes=[
            pltpu.VMEM((span // 2, 2 * keys), jnp.bfloat16),
            pltpu.VMEM((2 * keys, span), jnp.float32),
            pltpu.VMEM((span // 2, block), jnp.bfloat16),
        ],
        compiler_params=params(2, room=56),
        cost_estimate=lasting(20),
        name="attend_back",
    )(query, *sides, out, weights, inverse, near, far)


def middle_kernel(
    flags_ref, first_ref, second_ref, third_ref, fourth_ref, coded_ref, cot0_ref, cot1_ref, cot2_ref,
    cot3_ref, vec_ref, bias_ref, mine_ref, other_ref,
    back0_ref, back1_ref, back2_ref, back3_ref,
    hidden_ref, mixed_ref, upper_grad_ref, lowered_grad_ref, attn_ref, bias_grad_ref,
    out_weight_ref, down_ref, up_ref, cot_ref
):
    step = pl.program_id(0)

    @pl.when(step == 0)
    def _():
        width, slab = out_weight_ref.shape[1], up_ref.shape[1]
        core, chip = flags_ref[1], flags_ref[2]
        assembled(out_weight_ref, mine_ref, other_ref, chip, core, 0, width)
        assembled(up_ref, mine_ref, other_ref, 0, core, width, width + slab)
        assembled(down_ref, mine_ref, other_ref, 0, core, width + slab, None)

    unit = back0_ref.shape[0]
    share = cot_ref.shape[0] // unit
    for place, ref in enumerate((cot0_ref, cot1_ref, cot2_ref, cot3_ref)):

        @pl.when(step == place // share)
        def _(ref=ref, low=place % share * unit):
            cot_ref[low : low + unit, :] = ref[...]

    start = started(coded_ref[...].astype(jnp.float32), vec_ref[0:1, :])
    attns = []
    for place in range(share):
        own = step * share + place
        pieces = [
            ref[:, pl.ds(pl.multiple_of((own ^ flip) * unit, unit), unit)]
            for flip, ref in enumerate((first_ref, second_ref, third_ref, fourth_ref))
        ]
        attns.append(product(jnp.concatenate(pieces, 0), out_weight_ref[...], slim_form))
    attn = jnp.concatenate(attns, 0)

    @pl.when(step == 0)
    def _():
        attn_ref[...] = attns[0]
        bias_grad_ref[...] = jnp.zeros_like(bias_grad_ref)

    middle = start + vec_ref[4:5, :] * attn
    normed, _ = centered(middle)
    mixed = to_half(normed * vec_ref[5:6, :] * (1.0 + vec_ref[6:7, :]) + vec_ref[7:8, :])
    mixed_ref[...] = mixed
    upper = product(mixed, up_ref[...]) + bias_ref[...]
    square = upper * upper
    level = jnp.tanh(curve * upper * (1.0 + cube * square))
    hidden_ref[...] = to_half(0.5 * upper * (1.0 + level))
    slope = 0.5 * (1.0 + level) + (0.5 * curve) * upper * (1.0 - level * level) * (
        1.0 + (3.0 * cube) * square
    )
    lowered_grad = to_half(cot_ref[...].astype(jnp.float32) * vec_ref[8:9, :])
    lowered_grad_ref[...] = lowered_grad
    upper_grad = to_half(product(lowered_grad, down_ref[...], pair_form) * slope)
    upper_grad_ref[...] = upper_grad
    bias_grad_ref[0:1, :] += jnp.sum(upper_grad.astype(jnp.float32), 0, keepdims=True)
    back = to_half(product(upper_grad, up_ref[...], pair_form))
    for place, ref in enumerate((back0_ref, back1_ref, back2_ref, back3_ref)):

        @pl.when(step == place // share)
        def _(ref=ref, low=place % share * unit):
            ref[...] = back[low : low + unit, :]


def middle_stage(flags, outs, coded, cots, vectors, bias, mine, other, block):
    count, width = coded.shape
    hidden = bias.shape[1]
    row = pl.BlockSpec((block, width), lambda step: (step, 0))
    high = pl.BlockSpec((block, hidden), lambda step: (step, 0))
    unit = count // 4
    half = jnp.bfloat16
    return pl.pallas_call(
        middle_kernel,
        grid=(count // block,),
        in_specs=[pl.BlockSpec(memory_space=pltpu.SMEM)]
        + [whole(outs[0].shape)] * 4
        + [row]
        + [whole((unit, width))] * 4
        + [whole(vectors.shape), whole(bias.shape)]
        + [whole(mine.shape), whole(other.shape)],
        out_specs=[whole((unit, width))] * 4
        + [high, row, high, row, whole((unit, width)), whole((8, hidden))]
        + [whole((width, width)), whole((hidden, width))],
        out_shape=[jax.ShapeDtypeStruct((unit, width), half)] * 4
        + [
            jax.ShapeDtypeStruct((count, hidden), half),
            jax.ShapeDtypeStruct((count, width), half),
            jax.ShapeDtypeStruct((count, hidden), half),
            jax.ShapeDtypeStruct((count, width), half),
            jax.ShapeDtypeStruct((unit, width), jnp.float32),
            jax.ShapeDtypeStruct((8, hidden), jnp.float32),
            jax.ShapeDtypeStruct((width, width), half),
            jax.ShapeDtypeStruct((hidden, width), half),
        ],
        scratch_shapes=[pltpu.VMEM((width, hidden), half), pltpu.VMEM((block, width), half)],
        compiler_params=params(room=56),
        cost_estimate=lasting(15),
        name="middle",
    )(flags, *outs, coded, *cots, vectors, bias, mine, other)


def parted(grad_ref, core, kept_ref, sent_ref, low):
    chips = kept_ref.shape[0]
    size = grad_ref.shape[0] // (2 * chips)
    for chip in range(chips):
        base = 2 * chip * size
        mine = pl.multiple_of(base + core * size, size)
        theirs = pl.multiple_of(base + (1 - core) * size, size)
        kept_ref[chip, low : low + size, :] = grad_ref[pl.ds(mine, size), :]
        sent_ref[chip, low : low + size, :] = to_half(grad_ref[pl.ds(theirs, size), :])


def late_kernel(
    flags_ref, hidden_ref, mixed_ref, upper_grad_ref, lowered_grad_ref, down_ref,
    low0_ref, low1_ref, low2_ref, low3_ref, kept_ref, sent_ref, up_grad_ref, down_grad_ref
):
    step = pl.program_id(0)
    hidden, lowered_grad = hidden_ref[...], lowered_grad_ref[...]
    lowered = to_half(product(hidden, down_ref[...]))
    for place, ref in enumerate((low0_ref, low1_ref, low2_ref, low3_ref)):

        @pl.when(step == place)
        def _(ref=ref):
            ref[...] = lowered

    @pl.when(step == 0)
    def _():
        up_grad_ref[...] = jnp.zeros_like(up_grad_ref)
        down_grad_ref[...] = jnp.zeros_like(down_grad_ref)

    down_grad_ref[...] += product(hidden, lowered_grad, slim_form)
    up_grad_ref[...] += product(mixed_ref[...], upper_grad_ref[...], slim_form)

    @pl.when(step == pl.num_programs(0) - 1)
    def _():
        parted(up_grad_ref, flags_ref[1], kept_ref, sent_ref, 0)
        parted(down_grad_ref, flags_ref[1], kept_ref, sent_ref, kept_ref.shape[1] // 2)


def late_stage(flags, hidden, mixed, upper_grad, lowered_grad, down, block):
    count, width = mixed.shape
    slab = hidden.shape[1]
    row = pl.BlockSpec((block, width), lambda step: (step, 0))
    high = pl.BlockSpec((block, slab), lambda step: (step, 0))
    pile = (4, width // 4, width)
    return pl.pallas_call(
        late_kernel,
        grid=(count // block,),
        in_specs=[pl.BlockSpec(memory_space=pltpu.SMEM), high, row, high, row, whole(down.shape)],
        out_specs=[whole((block, width))] * 4 + [whole(pile)] * 2,
        out_shape=[jax.ShapeDtypeStruct((block, width), jnp.bfloat16)] * 4
        + [jax.ShapeDtypeStruct(pile, jnp.float32), jax.ShapeDtypeStruct(pile, jnp.bfloat16)],
        scratch_shapes=[
            pltpu.VMEM((width, slab), jnp.float32),
            pltpu.VMEM((slab, width), jnp.float32),
        ],
        compiler_params=params(room=56),
        cost_estimate=lasting(10),
        name="late",
    )(flags, hidden, mixed, upper_grad, lowered_grad, down)


def turn_kernel(
    flags_ref, own_ref, second_ref, third_ref, fourth_ref, coded_ref, cot_ref, attn_ref, vec_ref, out_weight_ref,
    out0_ref, out1_ref, out2_ref, out3_ref,
    middle_grad_ref, side0_ref, side1_ref, side2_ref, side3_ref, sums_ref, kept_ref, sent_ref,
    weight_grad_ref
):
    coded = coded_ref[...].astype(jnp.float32)
    start = started(coded, vec_ref[0:1, :])
    attn = attn_ref[...]
    middle = start + vec_ref[4:5, :] * attn
    normed, scale = centered(middle)
    grad = (
        own_ref[...].astype(jnp.float32)
        + second_ref[...].astype(jnp.float32)
        + third_ref[...].astype(jnp.float32)
        + fourth_ref[...].astype(jnp.float32)
    )
    swell = grad * (1.0 + vec_ref[6:7, :]) * vec_ref[5:6, :]
    level = jnp.mean(swell, -1, keepdims=True)
    slope = jnp.mean(swell * normed, -1, keepdims=True)
    middle_grad = cot_ref[...].astype(jnp.float32) + scale * (swell - level - normed * slope)
    middle_grad_ref[...] = middle_grad
    attn_grad = to_half(middle_grad * vec_ref[4:5, :])
    part = side0_ref.shape[0]
    for place, ref in enumerate((side0_ref, side1_ref, side2_ref, side3_ref)):
        ref[...] = to_half(
            product(out_weight_ref[place * part : (place + 1) * part, :], attn_grad, pair_form)
        )
    sums_ref[...] = jnp.concatenate(
        [
            jnp.sum(grad, 0, keepdims=True),
            jnp.sum(grad * normed, 0, keepdims=True),
            jnp.sum(middle_grad * attn, 0, keepdims=True),
            jnp.sum(jnp.where(coded > 1e29, middle_grad, 0.0), 0, keepdims=True),
            jnp.zeros((4, grad.shape[1]), jnp.float32),
        ],
        0,
    )
    for place, ref in enumerate((out0_ref, out1_ref, out2_ref, out3_ref)):
        low = pl.multiple_of((flags_ref[2] ^ place) * part, part)
        weight_grad_ref[pl.ds(low, part), :] = product(ref[...], attn_grad)
    parted(weight_grad_ref, flags_ref[1], kept_ref, sent_ref, 0)


def turn_stage(flags, backs, coded, cot, attn, vectors, out_weight, outs):
    count, width = attn.shape
    row = whole((count, width))
    part = outs[0].shape[0]
    sides = [
        pl.BlockSpec((part, count), functools.partial(lambda flip, step: (0, flip), flip))
        for flip in range(4)
    ]
    pile = (4, width // 8, width)
    return pl.pallas_call(
        turn_kernel,
        grid=(1,),
        in_specs=[pl.BlockSpec(memory_space=pltpu.SMEM)]
        + [row] * 7
        + [whole(vectors.shape), whole(out_weight.shape)]
        + sides,
        out_specs=[row] + [whole((part, count))] * 4 + [whole((8, width)), whole(pile), whole(pile)],
        out_shape=[jax.ShapeDtypeStruct((count, width), jnp.float32)]
        + [jax.ShapeDtypeStruct((part, count), jnp.bfloat16)] * 4
        + [
            jax.ShapeDtypeStruct((8, width), jnp.float32),
            jax.ShapeDtypeStruct(pile, jnp.float32),
            jax.ShapeDtypeStruct(pile, jnp.bfloat16),
        ],
        scratch_shapes=[pltpu.VMEM((width, width), jnp.float32)],
        compiler_params=params(room=56),
        cost_estimate=lasting(5),
        name="turn",
    )(flags, *backs, coded, cot, attn, vectors, out_weight, *outs)


def finish_kernel(
    flags_ref, low0_ref, low1_ref, low2_ref, low3_ref, coded_ref, cot_ref, attn_ref,
    lowered_grad_ref, vec_ref, turn_sums_ref, bias_ref, output_ref, sums_ref
):
    start = started(coded_ref[...].astype(jnp.float32), vec_ref[0:1, :])
    lowered = (
        low0_ref[...].astype(jnp.float32)
        + low1_ref[...].astype(jnp.float32)
        + low2_ref[...].astype(jnp.float32)
        + low3_ref[...].astype(jnp.float32)
        + vec_ref[9:10, :]
    )
    output = to_half(start + vec_ref[4:5, :] * attn_ref[...] + vec_ref[8:9, :] * lowered)
    rows = output_ref.shape[1]
    for order in range(output_ref.shape[0]):
        output_ref[flags_ref[0] ^ order] = output[order * rows : (order + 1) * rows, :]
    zero = jnp.zeros((1, lowered.shape[1]), jnp.float32)
    mlp_shift, mlp_scaled = turn_sums_ref[0:1, :], turn_sums_ref[1:2, :]
    sums_ref[...] = jnp.concatenate(
        [
            zero,
            zero,
            turn_sums_ref[2:3, :],
            mlp_shift,
            mlp_scaled * vec_ref[5:6, :],
            jnp.sum(cot_ref[...].astype(jnp.float32) * lowered, 0, keepdims=True),
            zero,
            mlp_scaled * (1.0 + vec_ref[6:7, :]),
            jnp.sum(lowered_grad_ref[...].astype(jnp.float32), 0, keepdims=True),
            turn_sums_ref[3:4, :],
        ]
        + [jnp.where(flags_ref[2] == order, bias_ref[0:1, :], 0.0) for order in range(4)]
        + [zero, zero],
        0,
    )


def finish_stage(
    flags, lows, coded, cot, attn, lowered_grad, vectors, turn_sums, bias_sums
):
    count, width = attn.shape
    row = whole((count, width))
    few = whole((8, width))
    return pl.pallas_call(
        finish_kernel,
        grid=(1,),
        in_specs=[pl.BlockSpec(memory_space=pltpu.SMEM)]
        + [row] * 8
        + [whole(vectors.shape), few, few],
        out_specs=[whole((4, count // 4, width)), whole((16, width))],
        out_shape=[
            jax.ShapeDtypeStruct((4, count // 4, width), jnp.bfloat16),
            jax.ShapeDtypeStruct((16, width), jnp.float32),
        ],
        compiler_params=params(room=56),
        cost_estimate=lasting(3),
        name="finish",
    )(flags, *lows, coded, cot, attn, lowered_grad, vectors, turn_sums, bias_sums)


def exit_kernel(
    flags_ref, query_ref, near_ref, far_ref, cos_ref, sin_ref, coded_ref, vec_ref, weight_ref,
    more_ref, mixed_ref, start_ref, sums_ref, kept_ref, sent_ref, packed_ref, grad_ref
):
    step = pl.program_id(0)
    cosine, sine = cos_ref[...], sin_ref[...]
    span = cosine.shape[1]
    wide = near_ref.shape[1]
    heads = wide // span
    lane = lax.broadcasted_iota(jnp.int32, cosine.shape, 1)
    queries = []
    for place in range(heads):
        low = place * span
        keys = near_ref[:, low : low + span] + far_ref[:, low : low + span].astype(jnp.float32)
        query = query_ref[:, low : low + span]
        packed_ref[:, low : low + span] = to_half(keys * cosine - half_turn(keys) * sine)
        queries.append(query * cosine - half_turn(query) * sine)
    for place in range(0, heads, 2):
        pair = queries[place]
        if place + 1 < heads:
            pair = jnp.where(lane < span // 2, pair, pltpu.roll(queries[place + 1], span // 2, 1))
        low = wide + place // 2 * span
        packed_ref[:, low : low + span] = to_half(pair)
    packed = packed_ref[...]
    part = product(mixed_ref[...], packed, slim_form)

    @pl.when(step == 0)
    def _():
        grad_ref[...] = part

    @pl.when(step > 0)
    def _():
        grad_ref[...] += part

    grad = product(packed, weight_ref[...], pair_form)
    coded = coded_ref[...].astype(jnp.float32)
    normed, scale = centered(started(coded, vec_ref[0:1, :]))
    swell = grad * (1.0 + vec_ref[2:3, :]) * vec_ref[1:2, :]
    level = jnp.mean(swell, -1, keepdims=True)
    slope = jnp.mean(swell * normed, -1, keepdims=True)
    start_grad = scale * (swell - level - normed * slope)
    block = start_ref.shape[1] - 2 * sums_ref.shape[0]
    share = start_grad.shape[0] // block
    for place in range(share):
        start_ref[flags_ref[2] ^ (share * step + place), :block, :] = to_half(
            start_grad[place * block : (place + 1) * block, :]
        )

    @pl.when(step == 0)
    def _():
        sums_ref[...] = more_ref[...]

    scaled = jnp.sum(grad * normed, 0, keepdims=True)
    sums_ref[0:1, :] += jnp.sum(grad, 0, keepdims=True)
    sums_ref[1:2, :] += scaled * vec_ref[1:2, :]
    sums_ref[6:7, :] += scaled * (1.0 + vec_ref[2:3, :])
    sums_ref[9:10, :] += jnp.sum(jnp.where(coded > 1e29, start_grad, 0.0), 0, keepdims=True)

    @pl.when(step == pl.num_programs(0) - 1)
    def _():
        rest = sums_ref[...]
        high = to_half(rest)
        both = jnp.concatenate([high, to_half(rest - high.astype(jnp.float32))], 0)
        for place in range(start_ref.shape[0]):
            start_ref[place, block:, :] = both
        parted(grad_ref, flags_ref[1], kept_ref, sent_ref, 0)


def exit_stage(
    flags, query_grad, near_grad, far_grad, cosine, sine, coded, vectors, weight, more, mixed,
    block
):
    count, width = coded.shape
    span = cosine.shape[1]
    wide = near_grad.shape[1]
    pack = weight.shape[1]
    pile = (4, count // 4 + 2 * more.shape[0], width)
    row = pl.BlockSpec((block, width), lambda step: (step, 0))
    table = pl.BlockSpec((block, span), lambda step: (step, 0))
    piece = pl.BlockSpec((block, wide), lambda step: (step, 0))
    cut = (4, width // 8, pack)
    return pl.pallas_call(
        exit_kernel,
        grid=(count // block,),
        in_specs=[pl.BlockSpec(memory_space=pltpu.SMEM)]
        + [piece, piece, piece, table, table, row, whole(vectors.shape), whole(weight.shape)]
        + [whole(more.shape), row],
        out_specs=[whole(pile), whole(more.shape), whole(cut), whole(cut)],
        out_shape=[
            jax.ShapeDtypeStruct(pile, jnp.bfloat16),
            jax.ShapeDtypeStruct(more.shape, jnp.float32),
            jax.ShapeDtypeStruct(cut, jnp.float32),
            jax.ShapeDtypeStruct(cut, jnp.bfloat16),
        ],
        scratch_shapes=[
            pltpu.VMEM((block, pack), jnp.bfloat16),
            pltpu.VMEM((width, pack), jnp.float32),
        ],
        compiler_params=params(room=56),
        cost_estimate=lasting(8),
        name="exit",
    )(flags, query_grad, near_grad, far_grad, cosine, sine, coded, vectors, weight, more, mixed)


def plane_shards(
    tokens,
    cotangent,
    time_index,
    absorbed,
    time_table,
    ada_weight,
    ada_bias,
    attn_gain,
    qkv_weight,
    out_weight,
    mlp_gain,
    up_weight,
    up_bias,
    down_weight,
    down_bias,
    mask_vector,
):
    batch, rows, width = tokens.shape
    layers, chips = lax.axis_size("fsdp"), lax.axis_size("chip")
    places = 2 * chips
    devices = layers * places
    head = width // H
    span = 2 * head
    heads = H // chips
    part = width // chips
    hidden = up_weight.shape[1]
    slab = hidden // layers
    slim = slab // chips
    count = rows * layers
    total = count * chips
    level = lax.axis_index("fsdp")
    chip = lax.axis_index("chip")
    core = lax.axis_index("core")
    place = 2 * chip + core
    wide = jnp.float32
    low_half = part // 2
    everyone = ("chip", "core", "fsdp")

    def across(value):
        return lax.all_to_all(value, "fsdp", 0, 0, tiled=True)

    def between(value):
        return lax.all_to_all(value, "chip", 0, 0, tiled=True)

    def through(value):
        pieces = [picked(value, level)] + [
            mirrored(picked(value, level ^ flip), "fsdp", flip) for flip in range(1, layers)
        ]
        return ordered(pieces, level)

    def ordered(pieces, spot):
        stack = jnp.stack(pieces)
        return jnp.stack([picked(stack, spot ^ order) for order in range(len(pieces))])

    def scattered(pieces):
        return [pieces[0]] + [mirrored(pieces[flip], "chip", flip) for flip in range(1, chips)]

    flags = jnp.stack([level, core, chip, place])
    small = [mask_vector, attn_gain, mlp_gain, down_bias, up_bias]
    packet, pack = prologue(
        flags, time_index, tokens, absorbed, time_table, small, qkv_weight
    )
    def half_rows(value):
        return lax.dynamic_slice_in_dim(value, core * low_half, low_half, 0)

    up_cut = picked(half_rows(up_weight).reshape(-1, 2 * layers, chips, slim // 2), chip, 2)
    up_cut = up_cut.reshape(-1, slab)
    down_cut = picked(down_weight.reshape(2, chips, -1, width), core)
    down_cut = picked(down_cut, chip)
    half = ada_weight.shape[0] // 2
    ada_cut = lax.dynamic_slice_in_dim(ada_weight, core * half, half, 0)
    ada_cut = jnp.swapaxes(ada_cut.reshape(half, 6, width), 0, 1).reshape(6 * half, width)
    dense = jnp.concatenate([half_rows(out_weight), up_cut, down_cut], 1)
    dense = jnp.broadcast_to(dense, (layers, *dense.shape))
    offsets = jnp.stack([(place ^ (2 * flip)) * count for flip in range(chips)])
    positions = (offsets[:, None] + jnp.arange(count, dtype=jnp.int32)[None, :]).reshape(-1)
    freqs = 10000.0 ** (-2.0 * jnp.arange(head // 2, dtype=wide) / head)
    angles = positions.astype(wide)[:, None] * freqs[None, :]
    cosine, sine = jnp.cos(angles), jnp.sin(angles)
    ones, zeros = jnp.ones((total, head), wide), jnp.zeros((total, head), wide)
    cosine = jnp.concatenate([cosine, cosine, ones], 1)
    sine = jnp.concatenate([-sine, sine, zeros], 1)

    packet, dense, cosine, sine = tied(across(packet), dense, cosine, sine)
    coded_own = packet[:, :rows].reshape(count, width)
    fields = packet[:, rows:].astype(wide)
    raw_time = jnp.sum(fields[:, :batch, : time_table.shape[1]], 0)
    mask_full, attn_gain_full, mlp_gain_full, down_bias_full = [
        fields[:, 8 + order, :part].reshape(-1) for order in range(4)
    ]
    up_bias_own = picked(fields[:, 12].reshape(layers, 2, chips, -1), chip, 2).reshape(-1)
    cond, silu_pull = jax.vjp(jax.nn.silu, raw_time)
    slice_rows = ada_weight.shape[0]
    cond_own = lax.dynamic_slice_in_dim(cond, level * slice_rows, slice_rows, 1)
    mod_part = jnp.dot(cond_own, ada_weight.astype(wide), precision=precise)
    bias_row = lax.dynamic_update_slice(
        jnp.zeros((mod_part.shape[1],), wide), ada_bias.astype(wide), (level * ada_bias.shape[0],)
    )
    mod_part = mod_part + bias_row[None, :]
    coded = scattered([coded_own] * chips)
    modulation = jnp.sum(across(mod_part), 0).reshape(6, width)
    shift_attn, scale_attn, gate_attn, shift_mlp, scale_mlp, gate_mlp = modulation
    vectors = jnp.stack(
        [
            mask_full,
            attn_gain_full,
            scale_attn,
            shift_attn,
            gate_attn,
            mlp_gain_full,
            scale_mlp,
            shift_mlp,
            gate_mlp,
            down_bias_full,
        ]
        + [jnp.zeros_like(mask_full)] * 6
    )

    pack, coded_own = tied(pack, coded_own)
    landed = [pack] + [mirrored(pack, "fsdp", flip) for flip in range(1, layers)]
    pack_mine = jnp.stack(landed)
    cot_source, vectors, pack_mine, *coded = tied(cotangent, vectors, pack_mine, *coded)
    cot_own = across(cot_source)
    pack_other = mirrored(pack_mine, "core", 1)
    mixed_attn, near, query, attn_weight, coded = entry(
        flags, coded, vectors, pack_mine, pack_other, cosine, sine, heads, total
    )
    near, dense, cot_own = tied(near, dense, cot_own)
    mine = across(dense)
    cot_own = cot_own.reshape(count, width)
    far = mirrored(near, "core", 1)
    far, cot_own = tied(far, cot_own)
    cots = scattered([cot_own] * chips)

    chunk = min(512, total)
    out, weights, inverse = attend(query, near, far, span, total // 2, chunk)
    out, *cots = tied(out, *cots)
    outs = scattered([out] * chips)
    mine, *outs = tied(mine, *outs)
    other = mirrored(mine, "core", 1)
    (
        back0, back1, back2, back3, hidden_own, mixed_mlp, upper_grad, lowered_grad, attn, bias_sum,
        out_full, down_full,
    ) = middle_stage(
        flags, outs, coded, cots, vectors, up_bias_own[None, :], mine, other, total
    )

    backs = scattered([back0, back1, back2, back3])
    ada_cut, hidden_own = tied(ada_cut, hidden_own)
    ada_mine = jnp.stack(
        [ada_cut] + [mirrored(ada_cut, "fsdp", flip) for flip in range(1, layers)]
    )
    backs[3], ada_mine = tied(backs[3], ada_mine)
    *lows, kept, sent = late_stage(
        flags, hidden_own, mixed_mlp, upper_grad, lowered_grad, down_full, count
    )
    landed = mirrored(sent, "core", 1)
    middle_grad, side0, side1, side2, side3, mlp_sums, out_kept, out_sent = turn_stage(
        flags, backs, coded_own, cot_own, attn, vectors, out_full, outs
    )
    sides = scattered([side0, side1, side2, side3])
    *lows, middle_grad = tied(*lows, middle_grad)
    out_landed = mirrored(out_sent, "core", 1)
    grads = to_half(
        jnp.concatenate(
            [kept + landed.astype(wide), out_kept + out_landed.astype(wide)], 1
        )
    )
    fine = width // devices
    edge = layers * fine

    def by_layer(value):
        return jnp.swapaxes(value.reshape(chips, layers, fine, -1), 0, 1).reshape(layers, edge, -1)

    grads = jnp.concatenate(
        [by_layer(grads[:, :edge]), by_layer(grads[:, 2 * edge :]), grads[:, edge : 2 * edge]], 1
    )
    query_late, grads = tied(query, grads)
    grads = across(grads)
    lowered_parts = scattered(lows)
    query_grad, near_grad, far_grad = attend_back(
        query_late, sides, out, weights, inverse, near, far, span, total, chunk // 2
    )
    far_grad, *lowered_parts = tied(far_grad, *lowered_parts)
    far_grad = mirrored(far_grad, "core", 1)
    output, sums = finish_stage(
        flags, lowered_parts, coded_own, cot_own, attn, lowered_grad, vectors, mlp_sums, bias_sum
    )
    far_grad, sums, output = tied(far_grad, sums, output)
    start_parts, sums, qkv_kept, qkv_sent = exit_stage(
        flags, query_grad, near_grad, far_grad, cosine, sine, coded, vectors, attn_weight, sums,
        mixed_attn, total
    )
    start_parts, grads, ada_mine = tied(start_parts, grads, ada_mine)
    ada_other = mirrored(ada_mine, "core", 1)
    start_pieces = between(start_parts)
    grad_qkv = qkv_kept + mirrored(qkv_sent, "core", 1).astype(wide)
    grad_qkv = to_half(grad_qkv).reshape(chips, layers, fine, -1)
    grad_qkv = [picked(grad_qkv, level, 1)] + [
        mirrored(picked(grad_qkv, level ^ flip, 1), "fsdp", flip) for flip in range(1, layers)
    ]
    grad_qkv = to_half(sum(piece.astype(wide) for piece in grad_qkv))
    output = [output[0]] + [mirrored(output[flip], "fsdp", flip) for flip in range(1, layers)]
    start_pieces, grad_qkv, *output = tied(start_pieces, grad_qkv, *output)
    sums = jnp.sum(start_pieces[:, count:].reshape(2 * chips, -1, width).astype(wide), 0)
    start_grad = middle_grad + jnp.sum(start_pieces[:, :count].astype(wide), 0)
    homing = across(to_half(start_grad).reshape(layers, rows, width))
    sums = sums + mirrored(sums, "core", 1)
    grads = to_half(jnp.sum(grads.astype(wide), 0))

    high = to_half(sums[:6])
    split = jnp.concatenate([high, to_half(sums[:6] - high.astype(wide))], 0)
    lifts = []
    for block in (ada_mine, ada_other):
        tile = block.reshape(-1, width)
        lift = product(tile, split, pair_form).reshape(layers, 6, half, 2, 6)
        lifts.append(sum(lift[:, order, :, :, order].sum(-1) for order in range(6)))
    lifts = [ordered(list(lift), level) for lift in lifts]
    lift = jnp.stack([jnp.where(core == 0, lifts[0], lifts[1]), jnp.where(core == 0, lifts[1], lifts[0])], 1)
    lift = jnp.pad(lift.reshape(1, -1), ((0, 0), (0, width - lift.size)))
    sums = jnp.concatenate([sums[:14], lift, sums[15:]], 0)

    swapped = []
    for order in range(chips):
        for side_of in range(2):
            for floor in range(layers):
                target = (floor * 2 + side_of) * layers + order
                swapped.append(((order * 2 + side_of) * layers + floor, target))
    grad_down = lax.ppermute(grads[2 * edge :], everyone, swapped).astype(wide)
    mixed_grads = jnp.swapaxes(grads[: 2 * edge].reshape(2, chips, fine, width), 0, 1)
    pack_width = grad_qkv.shape[-1]
    grad_qkv = jnp.pad(grad_qkv, ((0, 0), (0, 0), (0, width - pack_width)))
    mixed_grads = jnp.concatenate([mixed_grads.reshape(chips, 2 * fine, width), grad_qkv], 1)
    mixed_grads, sums = tied(mixed_grads, sums)
    landed = [picked(mixed_grads, chip)] + [
        mirrored(picked(mixed_grads, chip ^ flip), "chip", flip) for flip in range(1, chips)
    ]
    landed = ordered(landed, chip).astype(wide)
    grad_up = landed[:, :fine].reshape(chips, fine, 2 * layers, slim // 2)
    grad_up = jnp.transpose(grad_up, (1, 2, 0, 3)).reshape(fine, -1)
    grad_out_weight = jnp.sum(landed[:, fine : 2 * fine], 0)
    grad_qkv = landed[:, 2 * fine :, :pack_width]
    sums = ordered(
        [sums] + [mirrored(sums, "fsdp", flip) for flip in range(1, layers)], level
    )
    kv = grad_qkv[..., : heads * span].reshape(chips, fine, heads, 2, head)
    grad_qkv = jnp.stack(
        [
            grad_qkv[..., heads * span : heads * span + part],
            kv[..., 0, :].reshape(chips, fine, part),
            kv[..., 1, :].reshape(chips, fine, part),
        ]
    )
    grad_qkv = jnp.transpose(grad_qkv, (2, 0, 1, 3)).reshape(fine, -1)

    mod_full = sums[:, :6].reshape(batch, -1)
    ada_bias_full = jnp.sum(mod_full, 0)
    total_sums = jnp.sum(sums, 0)
    device = place * layers + level
    grad_attn_gain, grad_mlp_gain, grad_down_bias, grad_mask = lax.dynamic_slice_in_dim(
        total_sums[6:10], device * fine, fine, 1
    )
    share = mod_full.shape[1] // devices
    grad_ada_bias = lax.dynamic_slice_in_dim(ada_bias_full, device * share, share)
    grad_up_bias = lax.dynamic_slice(
        total_sums, (10 + level, place * (slim // 2)), (1, slim // 2)
    )[0]
    grad_cond = sums[:, 14, : cond.shape[1]]
    grad_raw = silu_pull(grad_cond)[0]
    cond_rows = cond.shape[1] // devices
    cond_cut = lax.dynamic_slice_in_dim(cond, device * cond_rows, cond_rows, 1)
    grad_ada_weight = jnp.dot(cond_cut.T, mod_full, precision=precise)
    table_rows = time_table.shape[0] * layers // devices
    picks = time_index[None, :] == (
        device * table_rows + jnp.arange(table_rows, dtype=jnp.int32)
    )[:, None]
    grad_table = jnp.dot(picks.astype(wide), grad_raw, precision=precise)
    output = ordered(output, level).astype(wide)
    grad_tokens = jnp.where((absorbed == 1)[..., None], 0.0, homing.astype(wide))
    return (
        output,
        grad_tokens,
        grad_table,
        grad_ada_weight,
        grad_ada_bias,
        grad_attn_gain,
        grad_qkv,
        grad_out_weight,
        grad_mlp_gain,
        grad_up,
        grad_up_bias,
        grad_down,
        grad_down_bias,
        grad_mask,
    )


def suits(mesh, tokens, up_weight):
    places, layers = mesh.shape["ctx"], mesh.shape["fsdp"]
    batch, count, width = tokens.shape
    return (
        places == 8
        and layers == 4
        and batch == layers
        and H % (places // 2) == 0
        and width == 64 * H
        and count == 256 * places
        and up_weight.shape[1] == layers * width
    )


def placed(body, mesh, ctx):
    both = (*ctx, "fsdp")
    rows, flat, cut = P(None, both, None), P(both), P(both, None)
    return jax.shard_map(
        body,
        mesh=mesh,
        in_specs=(
            rows,
            rows,
            P(),
            P(None, both),
            P("fsdp", None),
            P("fsdp", None),
            P("fsdp"),
            P("fsdp"),
            P("fsdp", None),
            P("fsdp", None),
            P("fsdp"),
            P("fsdp", None),
            P("fsdp"),
            P("fsdp", None),
            P("fsdp"),
            P("fsdp"),
        ),
        out_specs=(rows, rows, cut, cut, flat, flat, cut, cut, flat, cut, flat, cut, flat, flat),
        check_vma=False,
    )


def solution(mesh):
    def run(*arrays):
        if suits(mesh, arrays[0], arrays[11]):
            places, layers = mesh.shape["ctx"], mesh.shape["fsdp"]
            split = mesh.devices.reshape(places // 2, 2, layers)
            fine = Mesh(split, ("chip", "core", "fsdp"))
            return placed(plane_shards, fine, ("chip", "core"))(*arrays)
        return placed(ring_shards, mesh, ("ctx",))(*arrays)

    return run
```
